128 devices in a mesh: ctx: 32 (over x, z, core), head: 4 (over y).
Axes of the slice: x: 4, y: 4, z: 4, core: 2. Of those that a mesh axis runs over, the one named last changes fastest.
Arguments:
- query_proj: bfloat16 [4096, 4096], P('ctx', 'head'), may hold values from -4 to 4
- key_proj: bfloat16 [4096, 4096], P('ctx', 'head'), may hold values from -6 to 6
- value_proj: bfloat16 [4096, 4096], P('ctx', 'head'), may hold values from -6 to 6
- grad_out: bfloat16 [4096, 4096], P('ctx', 'head'), may hold values from -4 to 4
- out_proj: bfloat16 [4096, 4096], P('head'), may hold values from -0.09375 to 0.09375
- filters: bfloat16 [256, 4096], P('head'), may hold values from -1 to 1, as said below
- skip_gain: float32 [4096], P('head'), may hold values from 0.5 to 1.5
- doc_lengths: int32 [4], replicated, may hold values from 1 to 17, 32 in all
- group_of: int32 [4096], P('head'), may hold values from 0 to 255, as said below
Outputs:
- grad_query: bfloat16 [4096, 4096], P('ctx', 'head')
- grad_key: bfloat16 [4096, 4096], P('ctx', 'head')
- grad_filters: float32 [256, 4096], P('head', 'ctx')
The draws below stay inside these ranges and needn't reach their ends.
Inputs may be any that keep to these rules, and one draw needn't show every extreme that they name: `filters`: filter entries never above 1 in magnitude. `group_of`: each filter group is named by exactly 16 channels, and the channels of the k-th block of 1024 channels name only groups k * 64 to (k + 1) * 64 - 1.
All inputs are finite; a program needn't handle non-finite values.
Results may differ from the reference program's by a relative error of at most 0.005.
Values may be sent and summed in bfloat16 or wider, within the bound.
A program may use at most 128 MiB of HBM per device.

```python
import math
import jax
import jax.numpy as jnp
import numpy as np
from jax import lax

D = 4096
G = 256
TOK_DEV = 128
DOCS = 4
CDEV = 1024
GDEV = 64
CPG = 16
SPANS = 32
L = 4096
N_CTX = 32


def draw_filters(key, part):
    key_rate, key_noise = jax.random.split(key, 2)
    lags = jnp.arange(L, dtype=jnp.float32)
    decay = jnp.exp(jax.random.uniform(key_rate, (G,), jnp.float32, math.log(30.0), math.log(4.0 * L)))
    noise = jnp.clip(jax.random.normal(key_noise, (G, L), jnp.float32), -4.0, 4.0)
    scale = jnp.sqrt(1.0 / jnp.minimum(decay, 1.0 * L))
    values = noise * jnp.exp(-lags[None, :] / decay[:, None]) * scale[:, None]
    return jnp.clip(values, -1.0, 1.0).astype(jnp.bfloat16)


def draw_group_of(key, part):
    shards = D // CDEV
    keys = jax.random.split(jax.random.fold_in(key, 7), shards)
    perms = jax.vmap(lambda single: jax.random.permutation(single, CDEV))(keys)
    base = jnp.arange(shards, dtype=jnp.int32)[:, None] * GDEV
    return (base + perms.astype(jnp.int32) // CPG).reshape(D).astype(jnp.int32)


def shard_levels(rng, shape, cuts, smallest, high):
    gain = 1.0
    for position, shards_of in cuts:
        heights = jax.random.uniform(jax.random.fold_in(jax.random.fold_in(rng, 6), position), (shards_of,), jnp.float32, smallest / len(cuts), high / len(cuts))
        gain = gain * jnp.repeat(jnp.exp(heights), shape[position] // shards_of).reshape((-1,) + (1,) * (len(shape) - 1 - position))
    return gain


def split_up(amount, total, limit, lean):
    loads = [(1 << 20) // math.isqrt(rank ** lean) + 1 for rank in range(2, amount + 1)]
    rest, holding = total - limit - (amount - 1), [1] * (amount - 1)
    while rest > 0:
        free = [i for i in range(amount - 1) if holding[i] < limit]
        pool, remaining = sum([loads[i] for i in free]), rest
        for i in free:
            more = min(limit - holding[i], max(1, remaining * loads[i] // pool), rest)
            holding[i] = holding[i] + more
            rest = rest - more
    return np.array([limit] + holding)


def uneven(rng, amount, total, bound, skew):
    if amount == 2:
        one = jax.random.randint(rng, (), max(1, total - bound), min(bound, total - 1) + 1)
        return jnp.stack([one, total - one])
    lengths = jnp.asarray(split_up(amount, total, bound, skew), jnp.int32)
    twos = (amount - 1) // 2
    donor, receiver = lengths[1:1 + 2 * twos:2], lengths[2:2 + 2 * twos:2]
    slack = jnp.minimum(donor - 1, bound - receiver)
    shifted = jax.random.randint(jax.random.fold_in(rng, 1), (twos,), 0, 1 << 20) % (slack + 1)
    lengths = lengths.at[1:1 + 2 * twos:2].set(donor - shifted).at[2:2 + 2 * twos:2].set(receiver + shifted)
    return lengths[jax.random.permutation(jax.random.fold_in(rng, 2), amount)]


def bell_draw(own_key, dims, width, bound, cuts=(), kind=jnp.bfloat16):
    array = width * jax.random.normal(own_key, dims, jnp.float32)
    if cuts:
        array = array * shard_levels(own_key, dims, cuts, -0.22, 0.18)
    return jnp.clip(array, -bound, bound).astype(kind)


def setup_inputs(seed: int = 0) -> dict:
    splits = jax.random.split(jax.random.key(seed), 10)
    return {
        "query_proj": bell_draw(splits[0], (L, D), 0.25, 4.0, ((0, 32), (1, 4))),
        "key_proj": bell_draw(splits[1], (L, D), 1.0, 6.0, ((0, 32), (1, 4))),
        "value_proj": bell_draw(splits[2], (L, D), 1.0, 6.0, ((0, 32), (1, 4))),
        "grad_out": bell_draw(splits[3], (L, D), 0.25, 4.0, ((0, 32), (1, 4))),
        "out_proj": bell_draw(splits[4], (D, D), D ** -0.5, 0.09375, ((0, 4),)),
        "filters": draw_filters(jax.random.fold_in(splits[9], 71), 0),
        "skip_gain": jnp.clip(0.5 + 1.0 * jax.random.uniform(splits[6], (D,), jnp.float32) ** shard_levels(splits[6], (D,), ((0, 4),), -0.2, 0.2), 0.5, 1.5),
        "doc_lengths": uneven(splits[7], DOCS, SPANS, SPANS // 2 + 1, 0).astype(jnp.int32),
        "group_of": draw_group_of(jax.random.fold_in(splits[9], 71), 0),
    }


def reference(query_proj, key_proj, value_proj, grad_out, out_proj, filters, skip_gain, doc_lengths, group_of):
    length = TOK_DEV * N_CTX
    feature_grad = jnp.dot(grad_out, out_proj.T, preferred_element_type=jnp.float32)
    conv_grad = (feature_grad * value_proj.astype(jnp.float32)).astype(jnp.bfloat16)
    gated = (query_proj.astype(jnp.float32) * key_proj.astype(jnp.float32)).astype(jnp.bfloat16)
    conv_grad, gated = lax.optimization_barrier((conv_grad, gated))
    conv_grad = conv_grad.astype(jnp.float32)
    gated = gated.astype(jnp.float32)
    span_index = (jnp.arange(length) // TOK_DEV).astype(jnp.int32)
    bounds = jnp.cumsum(doc_lengths).astype(jnp.int32)
    token_doc = jnp.sum((bounds[None, :] <= span_index[:, None]).astype(jnp.int32), axis=1)
    doc_masks = (token_doc[None, :] == jnp.arange(DOCS, dtype=jnp.int32)[:, None]).astype(jnp.float32)
    filt = filters.astype(jnp.float32)
    block_cols = min(256, D)
    blocks = D // block_cols
    stacked = (conv_grad.T.reshape(blocks, block_cols, length), gated.T.reshape(blocks, block_cols, length),
               query_proj.astype(jnp.float32).T.reshape(blocks, block_cols, length),
               key_proj.astype(jnp.float32).T.reshape(blocks, block_cols, length),
               group_of.reshape(blocks, block_cols), skip_gain.reshape(blocks, block_cols))

    def one_block(filter_grad, entry):
        grad_rows, gate_rows, query_rows, key_rows, group_rows, skip_rows = entry
        channel_filt = jnp.take(filt, group_rows, axis=0)
        filt_spec = jnp.fft.rfft(channel_filt, n=2 * length)
        gated_grad = jnp.zeros((block_cols, length), jnp.float32)
        lag_sums = jnp.zeros((block_cols, length), jnp.float32)
        for doc_index in range(DOCS):
            grad_doc = grad_rows * doc_masks[doc_index]
            gate_doc = gate_rows * doc_masks[doc_index]
            grad_spec = jnp.fft.rfft(grad_doc, n=2 * length)
            back = jnp.fft.irfft(grad_spec * jnp.conj(filt_spec), n=2 * length)[:, :length]
            gated_grad = gated_grad + back.astype(jnp.float32) * doc_masks[doc_index]
            corr = jnp.fft.irfft(grad_spec * jnp.conj(jnp.fft.rfft(gate_doc, n=2 * length)), n=2 * length)[:, :length]
            lag_sums = lag_sums + corr.astype(jnp.float32)
        gated_grad = gated_grad + skip_rows[:, None] * grad_rows
        query_out = (gated_grad * key_rows).astype(jnp.bfloat16)
        key_out = (gated_grad * query_rows).astype(jnp.bfloat16)
        onehot = (group_rows[None, :] == jnp.arange(G, dtype=jnp.int32)[:, None]).astype(jnp.float32)
        filter_grad = filter_grad + jnp.dot(onehot, lag_sums, precision=lax.Precision.HIGHEST)
        return filter_grad, (query_out, key_out)

    grad_filters, outs = lax.scan(one_block, jnp.zeros((G, length), jnp.float32), stacked)
    grad_query = outs[0].reshape(D, length).T
    grad_key = outs[1].reshape(D, length).T
    return grad_query, grad_key, grad_filters
```

```python
import jax
import jax.numpy as jnp
from jax import lax
from jax.experimental import pallas as pl
from jax.experimental.pallas import tpu as pltpu
from jax.sharding import PartitionSpec as P

TOK = 128
SPANS = 32
HEADS = 4
CH = 1024
GROUPS = 64
PER = 16
OWN = GROUPS // SPANS
LAGS = 17
KW = LAGS * TOK
HALF = TOK // 2
MESH = pl.DeviceIdType.MESH
F32 = jnp.float32
BF16 = jnp.bfloat16


def dot(a, b, ca, cb):
    return lax.dot_general(a, b, (((ca,), (cb,)), ((), ())), preferred_element_type=F32)


def iota(shape, dim):
    return lax.broadcasted_iota(jnp.int32, shape, dim)


def kernel(
    doc, go, q, k, v, w, filt, grp, skip,
    gq, gk, gf,
    gov, qv, kv, vv, wv, fv, perm, fg, conv, rem, gs, gr, xs, xr, ys, yr, toep, amat, gt, fs, fr,
    loc, ag_send, ag_recv, ex_send, ex_recv,
):
    i = lax.axis_index("ctx")
    h = lax.axis_index("head")
    up = lax.rem(h + 1, HEADS)
    down = lax.rem(h + HEADS - 1, HEADS)
    across = lax.rem(h + 2, HEADS)

    loads = [pltpu.make_async_copy(go, gov.at[0], loc.at[0])]
    loads.append(pltpu.make_async_copy(q, qv, loc.at[1]))
    loads.append(pltpu.make_async_copy(k, kv, loc.at[2]))
    loads.append(pltpu.make_async_copy(v, vv, loc.at[3]))
    loads.append(pltpu.make_async_copy(filt.at[:, pl.ds(0, KW)], fv, loc.at[4]))
    for slot, block in enumerate((h, down, up, across)):
        columns = pl.ds(pl.multiple_of(block * CH, CH), CH)
        loads.append(pltpu.make_async_copy(w.at[:, columns], wv.at[slot], loc.at[5 + slot]))
    for load in loads:
        load.start()

    barrier = pltpu.get_barrier_semaphore()
    pl.semaphore_signal(barrier, inc=1, device_id={"head": up}, device_id_type=MESH)
    pl.semaphore_signal(barrier, inc=1, device_id={"head": down}, device_id_type=MESH)

    def greet(n, carry):
        pl.semaphore_signal(barrier, inc=1, device_id={"ctx": lax.rem(i + n, SPANS)}, device_id_type=MESH)
        return carry

    lax.fori_loop(1, SPANS, greet, 0)
    pl.semaphore_wait(barrier, SPANS + 1)

    low, high = pl.ds(0, HALF), pl.ds(HALF, HALF)

    def over_head(n, src, dst, to):
        return pltpu.make_async_remote_copy(
            src, dst, ag_send.at[n], ag_recv.at[n], device_id={"head": to}, device_id_type=MESH
        )

    gather = [
        over_head(0, go.at[low], gov.at[1, low], up),
        over_head(1, go.at[high], gov.at[2, high], down),
        over_head(2, go.at[high], gov.at[1, high], up),
        over_head(3, go.at[low], gov.at[2, low], down),
        over_head(4, gov.at[1, low], gov.at[3, low], up),
        over_head(5, gov.at[2, high], gov.at[3, high], down),
    ]
    for n in range(4):
        gather[n].start()

    def exchange(n, src, dst, to):
        return pltpu.make_async_remote_copy(
            src, dst, ex_send.at[n], ex_recv.at[n], device_id={"ctx": to}, device_id_type=MESH
        )

    def scatter(n, src, dst):
        def send(step, carry):
            to = lax.rem(i + step, SPANS)
            exchange(n, src.at[to], dst.at[i], to).start()
            return carry

        lax.fori_loop(1, SPANS, send, 0)
        dst[i] = src[i]

    def arrived(n, src, dst):
        exchange(n, src.at[pl.ds(0, SPANS - 1)], dst.at[pl.ds(0, SPANS - 1)], i).wait_recv()

    def sent(n, src, dst):
        exchange(n, src.at[pl.ds(0, SPANS - 1)], dst.at[pl.ds(0, SPANS - 1)], i).wait_send()

    local = grp[...] - h * GROUPS
    before = jnp.where(iota((TOK, TOK), 0) < iota((TOK, TOK), 1), 1.0, 0.0).astype(BF16)
    names = iota((GROUPS, TOK), 0)
    total = jnp.zeros((GROUPS, 1), F32)
    for b in range(CH // TOK):
        row = local[b : b + 1, :]
        hot = jnp.where(names == row, 1.0, 0.0)
        count = jnp.sum(hot * (dot(hot.astype(BF16), before, 1, 0) + total), axis=0, keepdims=True)
        total = total + jnp.sum(hot, axis=1, keepdims=True)
        rank = row * PER + count.astype(jnp.int32)
        for r in range(CH // TOK):
            perm[r * TOK : (r + 1) * TOK, b * TOK : (b + 1) * TOK] = jnp.where(
                iota((TOK, TOK), 0) + r * TOK == rank, 1.0, 0.0
            ).astype(BF16)

    def permuted(rows, out):
        def tile(n, carry):
            part = dot(perm[pl.ds(pl.multiple_of(n * 256, 256), 256), :], rows, 1, 1)
            out[pl.ds(n * 8, 8)] = part.astype(BF16).reshape(8, OWN, PER, TOK)
            return carry

        lax.fori_loop(0, CH // 256, tile, 0)

    loads[1].wait()
    loads[2].wait()
    gated = (qv[...].astype(F32) * kv[...].astype(F32)).astype(BF16)
    permuted(gated, gs)
    scatter(0, gs, gr)

    block = lax.shift_right_logical(iota((SPANS * PER, TOK), 0), 4)
    ends = [doc[0]]
    for n in range(1, 4):
        ends.append(ends[-1] + doc[n])
    end = jnp.where(block < ends[0], ends[0], jnp.where(block < ends[1], ends[1], jnp.where(block < ends[2], ends[2], ends[3])))
    rem[...] = (end - block).astype(F32).astype(BF16).reshape(SPANS, PER, TOK)
    xr[pl.ds(SPANS, LAGS - 1)] = jnp.zeros((LAGS - 1, OWN, PER, TOK), BF16)

    gather[0].wait_recv()
    gather[4].start()
    gather[1].wait_recv()
    gather[5].start()

    def features(slot, first=False):
        def tile(n, carry):
            at = pl.ds(pl.multiple_of(n * 256, 256), 256)
            part = dot(gov[slot], wv[slot, at, :], 1, 1)
            fg[:, at] = part if first else fg[:, at] + part
            return carry

        lax.fori_loop(0, CH // 256, tile, 0)

    loads[0].wait()
    loads[5].wait()
    features(0, True)

    loads[4].wait()
    for u in range(OWN):
        pick = jnp.where(iota((PER, GROUPS), 1) == i * OWN + u, 1.0, 0.0).astype(BF16)
        line = dot(pick, fv[...], 1, 0)
        line = jnp.concatenate([line, jnp.zeros((PER, TOK), F32)], axis=1)
        for c in range(TOK // PER):
            turned = pltpu.roll(line, c * PER, 1, stride=1, stride_axis=0)
            toep[u, c * PER : (c + 1) * PER, :] = turned[:, :KW].astype(BF16)

    gather[2].wait_recv()
    loads[6].wait()
    features(1)
    gather[3].wait_recv()
    loads[7].wait()
    features(2)

    arrived(0, gs, gr)
    flip = jnp.where(iota((TOK, TOK), 0) + iota((TOK, TOK), 1) == TOK - 1, 1.0, 0.0).astype(BF16)
    for u in range(OWN):
        gt[u] = dot(flip, gr[:, u].reshape(SPANS * PER, TOK), 1, 1).astype(BF16)

    gather[4].wait_recv()
    gather[5].wait_recv()
    loads[8].wait()
    features(3)

    loads[3].wait()
    conv[...] = (fg[...] * vv[...].astype(F32)).astype(BF16)
    permuted(conv[...], xs)
    scatter(1, xs, xr)
    arrived(1, xs, xr)

    for u in range(OWN):
        for d in range(LAGS):
            part = jnp.where(rem[...] > d, xr[d : d + SPANS, u], jnp.zeros((), BF16))
            amat[u, :, d * TOK : (d + 1) * TOK] = part.reshape(SPANS * PER, TOK)
        ys[:, u] = dot(amat[u], toep[u], 1, 1).astype(BF16).reshape(SPANS, PER, TOK)
    scatter(2, ys, yr)

    sums = []
    for u in range(OWN):
        acc = jnp.zeros((PER, KW + TOK), F32)
        for c in range(TOK // PER):
            corr = dot(gt[u, c * PER : (c + 1) * PER, :], amat[u], 1, 0)
            corr = jnp.concatenate([corr, jnp.zeros((PER, TOK), F32)], axis=1)
            acc = acc + pltpu.roll(corr, 1 + c * PER, 1, stride=1, stride_axis=0)
        sums.append(jnp.sum(acc, axis=0, keepdims=True)[:, TOK:])
    place = iota((8, TOK), 0) - lax.rem(i, 4) * OWN
    for d in range(LAGS):
        at = slice(d * TOK, (d + 1) * TOK)
        fs[d] = jnp.where(place == 0, sums[0][:, at], jnp.where(place == 1, sums[1][:, at], 0.0))

    def lags_out(step, carry):
        to = lax.rem(i + step, SPANS)

        @pl.when(to < LAGS)
        def _():
            exchange(3, fs.at[to], fr.at[i], to).start()

        return carry

    lax.fori_loop(1, SPANS, lags_out, 0)

    arrived(2, ys, yr)
    for n in range(CH // 256):
        at = slice(n * 256, (n + 1) * 256)
        grad = dot(yr[...].reshape(CH, TOK), perm[:, at], 0, 0)
        grad = grad + skip[:, at] * conv[:, at].astype(F32)
        gq[:, at] = (grad * kv[:, at].astype(F32)).astype(BF16)
        gk[:, at] = (grad * qv[:, at].astype(F32)).astype(BF16)

    @pl.when(i < LAGS)
    def _():
        fr[i] = fs[i]
        arrived(3, fr, fr)
        for n in range(GROUPS // 8):
            gf[n * 8 : (n + 1) * 8, :] = (fr[4 * n] + fr[4 * n + 1]) + (fr[4 * n + 2] + fr[4 * n + 3])
        exchange(3, fs.at[pl.ds(0, LAGS - 1)], fr.at[pl.ds(0, LAGS - 1)], i).wait_send()

    @pl.when(i >= LAGS)
    def _():
        gf[...] = jnp.zeros((GROUPS, TOK), F32)
        exchange(3, fs, fr.at[pl.ds(0, LAGS)], i).wait_send()

    for copy in gather:
        copy.wait_send()
    sent(0, gs, gr)
    sent(1, xs, xr)
    sent(2, ys, yr)


def per_device(
    query_proj, key_proj, value_proj, grad_out, out_proj, filters, skip_gain, doc_lengths, group_of
):
    hbm = pl.BlockSpec(memory_space=pl.ANY)
    vmem = pl.BlockSpec(memory_space=pltpu.VMEM)
    smem = pl.BlockSpec(memory_space=pltpu.SMEM)
    dma = pltpu.SemaphoreType.DMA
    blocks = (SPANS, OWN, PER, TOK)
    return pl.pallas_call(
        kernel,
        out_shape=(
            jax.ShapeDtypeStruct((TOK, CH), BF16),
            jax.ShapeDtypeStruct((TOK, CH), BF16),
            jax.ShapeDtypeStruct((GROUPS, TOK), F32),
        ),
        in_specs=[smem, hbm, hbm, hbm, hbm, hbm, hbm, vmem, vmem],
        out_specs=(vmem, vmem, vmem),
        scratch_shapes=[
            pltpu.VMEM((HEADS, TOK, CH), BF16),
            pltpu.VMEM((TOK, CH), BF16),
            pltpu.VMEM((TOK, CH), BF16),
            pltpu.VMEM((TOK, CH), BF16),
            pltpu.VMEM((HEADS, CH, CH), BF16),
            pltpu.VMEM((GROUPS, KW), BF16),
            pltpu.VMEM((CH, CH), BF16),
            pltpu.VMEM((TOK, CH), F32),
            pltpu.VMEM((TOK, CH), BF16),
            pltpu.VMEM((SPANS, PER, TOK), BF16),
            pltpu.VMEM(blocks, BF16),
            pltpu.VMEM(blocks, BF16),
            pltpu.VMEM(blocks, BF16),
            pltpu.VMEM((SPANS + LAGS - 1, OWN, PER, TOK), BF16),
            pltpu.VMEM(blocks, BF16),
            pltpu.VMEM(blocks, BF16),
            pltpu.VMEM((OWN, TOK, KW), BF16),
            pltpu.VMEM((OWN, SPANS * PER, KW), BF16),
            pltpu.VMEM((OWN, TOK, SPANS * PER), BF16),
            pltpu.VMEM((LAGS, 8, TOK), F32),
            pltpu.VMEM((SPANS, 8, TOK), F32),
            dma((9,)),
            dma((6,)),
            dma((6,)),
            dma((4,)),
            dma((4,)),
        ],
        compiler_params=pltpu.CompilerParams(
            collective_id=0, has_side_effects=True, vmem_limit_bytes=48 << 20
        ),
    )(
        doc_lengths, grad_out, query_proj, key_proj, value_proj, out_proj, filters,
        group_of.reshape(CH // TOK, TOK), skip_gain.reshape(1, CH),
    )


def solution(mesh):
    in_specs = (
        P("ctx", "head"),
        P("ctx", "head"),
        P("ctx", "head"),
        P("ctx", "head"),
        P("head", None),
        P("head", None),
        P("head"),
        P(),
        P("head"),
    )
    out_specs = (P("ctx", "head"), P("ctx", "head"), P("head", "ctx"))
    return jax.shard_map(
        per_device, mesh=mesh, in_specs=in_specs, out_specs=out_specs, check_vma=False
    )
```

```python
import jax
import jax.numpy as jnp
from jax import lax
from jax.experimental import pallas as pl
from jax.experimental.pallas import tpu as pltpu
from jax.sharding import PartitionSpec as P

TOK = 128
SPANS = 32
HEADS = 4
CH = 1024
GROUPS = 64
PER = 16
OWN = GROUPS // SPANS
LAGS = 17
KW = LAGS * TOK
HALF = SPANS // 2
PIECE = CH // 4
ROWS = SPANS * PER
MESH = pl.DeviceIdType.MESH
F32 = jnp.float32
BF16 = jnp.bfloat16


def dot(a, b, ca, cb):
    return lax.dot_general(a, b, (((ca,), (cb,)), ((), ())), preferred_element_type=F32)


def iota(shape, dim):
    return lax.broadcasted_iota(jnp.int32, shape, dim)


def kernel(
    doc_in, go, q, k, v, w, filt, grp_in, skip_in,
    yr, perm, conv, qv, kv, skip, fr,
    own, gov, vv, wv, fv, grp, doc, fg, rem, gs, gr, xs, xr, ys, toep, amat, gt, corr, fs,
    loc, ag_send, ag_recv, ex_send, ex_recv,
):
    i = lax.axis_index("ctx")
    h = lax.axis_index("head")
    up = lax.rem(h + 1, HEADS)
    down = lax.rem(h + HEADS - 1, HEADS)
    across = lax.rem(h + 2, HEADS)
    x, z, core = i // 8, lax.rem(i // 2, 4), lax.rem(i, 2)

    barrier = pltpu.get_barrier_semaphore()
    pl.semaphore_signal(barrier, inc=1, device_id={"head": up}, device_id_type=MESH)
    pl.semaphore_signal(barrier, inc=1, device_id={"head": down}, device_id_type=MESH)

    def greet(n, carry):
        pl.semaphore_signal(barrier, inc=1, device_id={"ctx": lax.rem(i + n, SPANS)}, device_id_type=MESH)
        return carry

    lax.fori_loop(1, SPANS, greet, 0)

    pairs = [(grp_in, grp), (go, own), (q, qv), (k, kv), (doc_in, doc), (filt.at[:, pl.ds(0, KW)], fv), (v, vv), (skip_in, skip)]
    for slot, block in enumerate((h, down, up, across)):
        pairs.append((w.at[:, pl.ds(pl.multiple_of(block * CH, CH), CH)], wv.at[slot]))
    loads = [pltpu.make_async_copy(src, dst, loc.at[n]) for n, (src, dst) in enumerate(pairs)]
    for load in loads:
        load.start()
    l_grp, l_own, l_q, l_k, l_doc, l_filt, l_v, l_skip = loads[:8]
    l_w = loads[8:]
    pl.semaphore_wait(barrier, SPANS + 1)

    def over_head(n, src, dst, to, first, count):
        at = pl.ds(first * PIECE, count * PIECE)
        return pltpu.make_async_remote_copy(
            src.at[:, at], dst.at[:, at], ag_send.at[n], ag_recv.at[n], device_id={"head": to}, device_id_type=MESH
        )

    to_up = [over_head(0, go, gov.at[0], up, 0, 1), over_head(1, go, gov.at[0], up, 1, 1), over_head(2, go, gov.at[0], up, 2, 2)]
    to_down = [over_head(3, go, gov.at[1], down, 2, 1), over_head(4, go, gov.at[1], down, 3, 1), over_head(5, go, gov.at[1], down, 0, 2)]
    on_up = [over_head(6 + n, gov.at[0], gov.at[2], up, n, 1) for n in range(2)]
    on_down = [over_head(8 + n, gov.at[1], gov.at[2], down, 2 + n, 1) for n in range(2)]
    for n in range(2):
        to_up[n].start()
        to_down[n].start()

    flips = {0: x, 1: x + 1 - 2 * lax.rem(x, 2), 2: lax.rem(x + 2, 4), 3: 3 - x}
    turns = {0: z, 1: z + 1 - 2 * lax.rem(z, 2), 2: lax.rem(z + 2, 4), 3: 3 - z}
    hops = {0: 0, 1: 1, 2: 2, 3: 1}
    sides = []
    for side in ((2, 3), (1, 0)):
        steps = [(a, b, c) for a in side for b in range(4) for c in range(2) if a or b or c]
        steps.sort(key=lambda e: -hops[e[0]] - hops[e[1]])
        sides.append([flips[a] * 8 + turns[b] * 2 + (core if c == 0 else 1 - core) for a, b, c in steps])
    halves = (1 - x // 2, x // 2)

    def exchange(n, src, dst, to):
        return pltpu.make_async_remote_copy(
            src, dst, ex_send.at[n], ex_recv.at[n], device_id={"ctx": to}, device_id_type=MESH
        )

    def everything(n, src, dst):
        return exchange(n, src.at[pl.ds(0, SPANS - 1)], dst.at[pl.ds(0, SPANS - 1)], i)

    l_grp.wait()
    local = grp[...] - h * GROUPS
    before = jnp.where(iota((TOK, TOK), 0) < iota((TOK, TOK), 1), 1.0, 0.0).astype(BF16)
    names = iota((GROUPS, TOK), 0)
    total = jnp.zeros((GROUPS, 1), F32)
    for b in range(CH // TOK):
        row = local[b : b + 1, :]
        hot = jnp.where(names == row, 1.0, 0.0)
        count = jnp.sum(hot * (dot(hot.astype(BF16), before, 1, 0) + total), axis=0, keepdims=True)
        total = total + jnp.sum(hot, axis=1, keepdims=True)
        rank = (row & (OWN - 1)) * ROWS + lax.shift_right_logical(row, 1) * PER + count.astype(jnp.int32)
        for r in range(CH // TOK):
            perm[r * TOK : (r + 1) * TOK, b * TOK : (b + 1) * TOK] = jnp.where(
                iota((TOK, TOK), 0) + r * TOK == rank, 1.0, 0.0
            ).astype(BF16)

    l_q.wait()
    l_k.wait()
    gated = (qv[...].astype(F32) * kv[...].astype(F32)).astype(BF16)
    for u in range(OWN):
        gs[u] = dot(perm[u * ROWS : (u + 1) * ROWS, :], gated, 1, 1).astype(BF16).reshape(SPANS, PER, TOK)
    for side in sides:
        for to in side:
            exchange(0, gs.at[:, to], gr.at[:, i], to).start()
    gr[:, i] = gs[:, i]

    to_up[2].start()
    to_down[2].start()

    def features(block, slot, first=False):
        def tile(n, carry):
            at = pl.ds(pl.multiple_of(n * 256, 256), 256)
            part = dot(block[...], wv[slot, at, :], 1, 1)
            fg[:, at] = part if first else fg[:, at] + part
            return carry

        lax.fori_loop(0, CH // 256, tile, 0)

    l_own.wait()
    l_w[0].wait()
    features(own, 0, True)

    for n in range(2):
        to_up[n].wait_recv()
        on_up[n].start()
        to_down[n].wait_recv()
        on_down[n].start()

    l_doc.wait()
    block = lax.shift_right_logical(iota((ROWS, TOK), 0), 4)
    ends = [doc[0]]
    for n in range(1, 4):
        ends.append(ends[-1] + doc[n])
    end = jnp.where(block < ends[0], ends[0], jnp.where(block < ends[1], ends[1], jnp.where(block < ends[2], ends[2], ends[3])))
    rem[...] = (end - block).astype(F32).astype(BF16).reshape(SPANS, PER, TOK)
    xr[:, SPANS:] = jnp.zeros((OWN, LAGS - 1, PER, TOK), BF16)
    corr[:, KW:] = jnp.zeros((TOK, TOK), F32)

    l_filt.wait()
    for u in range(OWN):
        pick = jnp.where(iota((PER, GROUPS), 1) == i * OWN + u, 1.0, 0.0).astype(BF16)
        line = dot(pick, fv[...], 1, 0)
        line = jnp.concatenate([line, jnp.zeros((PER, TOK), F32)], axis=1)
        for c in range(TOK // PER):
            turned = pltpu.roll(line, c * PER, 1, stride=1, stride_axis=0)
            toep[u, c * PER : (c + 1) * PER, :] = turned[:, :KW].astype(BF16)

    to_up[2].wait_recv()
    l_w[1].wait()
    features(gov.at[0], 1)
    to_down[2].wait_recv()
    l_w[2].wait()
    features(gov.at[1], 2)

    exchange(0, gs.at[:, pl.ds(0, SPANS - 1)], gr.at[:, pl.ds(0, SPANS - 1)], i).wait_recv()
    flip = jnp.where(iota((TOK, TOK), 0) + iota((TOK, TOK), 1) == TOK - 1, 1.0, 0.0).astype(BF16)
    for u in range(OWN):
        gt[u] = dot(flip, gr[u].reshape(ROWS, TOK), 1, 1).astype(BF16)

    l_w[3].wait()
    l_v.wait()
    far = gov.at[2]
    for n in range(2):
        on_up[n].wait_recv()
        on_down[n].wait_recv()
        one, two = pl.ds(n * PIECE, PIECE), pl.ds((2 + n) * PIECE, PIECE)

        def tile(m, carry):
            at = pl.ds(pl.multiple_of(m * 256, 256), 256)
            part = dot(far[:, one], wv[3, at, one], 1, 1) + dot(far[:, two], wv[3, at, two], 1, 1)
            if n == 0:
                fg[:, at] = fg[:, at] + part
            else:
                conv[:, at] = ((fg[:, at] + part) * vv[:, at].astype(F32)).astype(BF16)
            return carry

        lax.fori_loop(0, CH // 256, tile, 0)

    for u in range(OWN):
        for side, half in zip(sides, halves):
            at = pl.ds(pl.multiple_of(u * ROWS + half * (ROWS // 2), ROWS // 2), ROWS // 2)
            part = dot(perm[at, :], conv[...], 1, 1)
            xs[u, pl.ds(half * HALF, HALF)] = part.astype(BF16).reshape(HALF, PER, TOK)
            for to in side:
                exchange(1 + u, xs.at[u, to], xr.at[u, i], to).start()
        xr[u, i] = xs[u, i]

    for u in range(OWN):
        everything(1 + u, xs.at[u], xr.at[u]).wait_recv()
        for side, half in zip(sides, halves):
            rows = pl.ds(pl.multiple_of(half * (ROWS // 2), ROWS // 2), ROWS // 2)
            for d in range(LAGS):
                near = rem[pl.ds(half * HALF, HALF)] > d
                part = jnp.where(near, xr[u, pl.ds(half * HALF + d, HALF)], jnp.zeros((), BF16))
                amat[u, rows, d * TOK : (d + 1) * TOK] = part.reshape(ROWS // 2, TOK)
            part = dot(amat[u, rows, :], toep[u], 1, 1)
            ys[u, pl.ds(half * HALF, HALF)] = part.astype(BF16).reshape(HALF, PER, TOK)
            for to in side:
                exchange(3 + u, ys.at[u, to], yr.at[u, i], to).start()
        yr[u, i] = ys[u, i]

    for u in range(OWN):
        corr[:, :KW] = dot(gt[u], amat[u], 1, 0)
        acc = jnp.zeros((PER, KW + TOK), F32)
        for c in range(TOK // PER):
            acc = acc + pltpu.roll(corr[c * PER : (c + 1) * PER, :], 1 + c * PER, 1, stride=1, stride_axis=0)
        line = jnp.sum(acc, axis=0, keepdims=True)
        for d in range(LAGS):
            fs[d, u : u + 1, :] = line[:, (d + 1) * TOK : (d + 2) * TOK]

    def lags_out(step, carry):
        to = lax.rem(i + step, SPANS)

        @pl.when(to < LAGS)
        def _():
            exchange(5, fs.at[to], fr.at[i], to).start()

        return carry

    lax.fori_loop(1, SPANS, lags_out, 0)

    @pl.when(i < LAGS)
    def _():
        fr[i] = fs[i]
        everything(5, fr, fr).wait_recv()
        exchange(5, fs.at[pl.ds(0, LAGS - 1)], fr.at[pl.ds(0, LAGS - 1)], i).wait_send()

    @pl.when(i >= LAGS)
    def _():
        fr[...] = jnp.zeros(fr.shape, F32)
        exchange(5, fs, fr.at[pl.ds(0, LAGS)], i).wait_send()

    for copy in (*to_up, *to_down, *on_up, *on_down):
        copy.wait_send()
    exchange(0, gs.at[:, pl.ds(0, SPANS - 1)], gr.at[:, pl.ds(0, SPANS - 1)], i).wait_send()
    l_skip.wait()
    for u in range(OWN):
        everything(1 + u, xs.at[u], xr.at[u]).wait_send()
        everything(3 + u, ys.at[u], yr.at[u]).wait_send()
        everything(3 + u, ys.at[u], yr.at[u]).wait_recv()


def finish(yr, perm, conv, qv, kv, skip, fr, gq, gk, gf, out_q, out_k, out_f, sem):
    for t in range(SPANS):
        out_f[t * OWN : (t + 1) * OWN, :] = fr[t]
    copies = [pltpu.make_async_copy(out_f, gf, sem.at[0])]
    copies[0].start()
    for n in range(CH // 256):
        at = slice(n * 256, (n + 1) * 256)
        grad = dot(yr[...].reshape(CH, TOK), perm[:, at], 0, 0)
        grad = grad + skip[:, at] * conv[:, at].astype(F32)
        out_q[:, at] = (grad * kv[:, at].astype(F32)).astype(BF16)
        out_k[:, at] = (grad * qv[:, at].astype(F32)).astype(BF16)
        for m, (src, dst) in enumerate(((out_q, gq), (out_k, gk))):
            copies.append(pltpu.make_async_copy(src.at[:, at], dst.at[:, at], sem.at[1 + 2 * n + m]))
            copies[-1].start()
    for copy in copies:
        copy.wait()


def per_device(
    query_proj, key_proj, value_proj, grad_out, out_proj, filters, skip_gain, doc_lengths, group_of
):
    hbm = pl.BlockSpec(memory_space=pltpu.HBM)
    vmem = pl.BlockSpec(memory_space=pltpu.VMEM)
    dma = pltpu.SemaphoreType.DMA
    blocks = (OWN, SPANS, PER, TOK)
    rows = (TOK, CH)
    args = (
        doc_lengths, grad_out, query_proj, key_proj, value_proj, out_proj, filters,
        group_of.reshape(CH // TOK, TOK), skip_gain.reshape(1, CH),
    )
    held = pl.pallas_call(
        kernel,
        out_shape=(
            jax.ShapeDtypeStruct(blocks, BF16),
            jax.ShapeDtypeStruct((CH, CH), BF16),
            jax.ShapeDtypeStruct(rows, BF16),
            jax.ShapeDtypeStruct(rows, BF16),
            jax.ShapeDtypeStruct(rows, BF16),
            jax.ShapeDtypeStruct((1, CH), F32),
            jax.ShapeDtypeStruct((SPANS, OWN, TOK), F32),
        ),
        in_specs=[hbm] * 9,
        out_specs=(vmem,) * 7,
        scratch_shapes=[
            pltpu.VMEM(rows, BF16),
            pltpu.VMEM((HEADS - 1, *rows), BF16),
            pltpu.VMEM(rows, BF16),
            pltpu.VMEM((HEADS, CH, CH), BF16),
            pltpu.VMEM((GROUPS, KW), BF16),
            pltpu.VMEM((CH // TOK, TOK), jnp.int32),
            pltpu.SMEM((4,), jnp.int32),
            pltpu.VMEM(rows, F32),
            pltpu.VMEM((SPANS, PER, TOK), BF16),
            pltpu.VMEM(blocks, BF16),
            pltpu.VMEM(blocks, BF16),
            pltpu.VMEM(blocks, BF16),
            pltpu.VMEM((OWN, SPANS + LAGS - 1, PER, TOK), BF16),
            pltpu.VMEM(blocks, BF16),
            pltpu.VMEM((OWN, TOK, KW), BF16),
            pltpu.VMEM((OWN, ROWS, KW), BF16),
            pltpu.VMEM((OWN, TOK, ROWS), BF16),
            pltpu.VMEM((TOK, KW + TOK), F32),
            pltpu.VMEM((LAGS, OWN, TOK), F32),
            dma((12,)),
            dma((10,)),
            dma((10,)),
            dma((6,)),
            dma((6,)),
        ],
        compiler_params=pltpu.CompilerParams(
            collective_id=0, has_side_effects=True, vmem_limit_bytes=40 << 20
        ),
    )(*(pltpu.with_memory_space_constraint(arg, pltpu.HBM) for arg in args))
    return pl.pallas_call(
        finish,
        out_shape=(
            jax.ShapeDtypeStruct(rows, BF16),
            jax.ShapeDtypeStruct(rows, BF16),
            jax.ShapeDtypeStruct((GROUPS, TOK), F32),
        ),
        in_specs=[vmem] * 7,
        out_specs=(hbm,) * 3,
        scratch_shapes=[pltpu.VMEM(rows, BF16), pltpu.VMEM(rows, BF16), pltpu.VMEM((GROUPS, TOK), F32), dma((9,))],
        compiler_params=pltpu.CompilerParams(vmem_limit_bytes=16 << 20),
    )(*held)


def solution(mesh):
    in_specs = (
        P("ctx", "head"),
        P("ctx", "head"),
        P("ctx", "head"),
        P("ctx", "head"),
        P("head", None),
        P("head", None),
        P("head"),
        P(),
        P("head"),
    )
    out_specs = (P("ctx", "head"), P("ctx", "head"), P("head", "ctx"))
    return jax.shard_map(
        per_device, mesh=mesh, in_specs=in_specs, out_specs=out_specs, check_vma=False
    )
```

```python
import jax
import jax.numpy as jnp
from jax import lax
from jax.experimental import pallas as pl
from jax.experimental.pallas import tpu as pltpu
from jax.sharding import PartitionSpec as P

TOK = 128
SPANS = 32
HEADS = 4
CH = 1024
GROUPS = 64
PER = 16
OWN = GROUPS // SPANS
LAGS = 17
KW = LAGS * TOK
HALF = SPANS // 2
PIECE = CH // 8
ROWS = SPANS * PER
MESH = pl.DeviceIdType.MESH
F32 = jnp.float32
BF16 = jnp.bfloat16


def dot(a, b, ca, cb):
    return lax.dot_general(a, b, (((ca,), (cb,)), ((), ())), preferred_element_type=F32)


def iota(shape, dim):
    return lax.broadcasted_iota(jnp.int32, shape, dim)


def kernel(
    doc_in, go, q, k, v, w, filt, grp_in, skip_in,
    out_q, out_k, fr,
    yr, perm, conv, qv, kv, skip, own, gov, vv, wv, fv, grp, doc, fg, rem, gs, gr, xs, xr, ys, toep, amat, gt, corr, fs,
    loc, ag_send, ag_recv, ex_send, ex_recv,
):
    i = lax.axis_index("ctx")
    h = lax.axis_index("head")
    up = lax.rem(h + 1, HEADS)
    down = lax.rem(h + HEADS - 1, HEADS)
    across = lax.rem(h + 2, HEADS)
    x, z, core = i // 8, lax.rem(i // 2, 4), lax.rem(i, 2)

    barrier = pltpu.get_barrier_semaphore()
    pl.semaphore_signal(barrier, inc=1, device_id={"head": up}, device_id_type=MESH)
    pl.semaphore_signal(barrier, inc=1, device_id={"head": down}, device_id_type=MESH)

    def greet(n, carry):
        pl.semaphore_signal(barrier, inc=1, device_id={"ctx": lax.rem(i + n, SPANS)}, device_id_type=MESH)
        return carry

    lax.fori_loop(1, SPANS, greet, 0)

    pairs = [(grp_in, grp), (go, own), (q, qv), (k, kv), (doc_in, doc), (filt.at[:, pl.ds(0, KW)], fv), (v, vv), (skip_in, skip)]
    for slot, block in enumerate((h, down, up, across)):
        pairs.append((w.at[:, pl.ds(pl.multiple_of(block * CH, CH), CH)], wv.at[slot]))
    loads = [pltpu.make_async_copy(src, dst, loc.at[n]) for n, (src, dst) in enumerate(pairs)]
    for load in loads:
        load.start()
    l_grp, l_own, l_q, l_k, l_doc, l_filt, l_v, l_skip = loads[:8]
    l_w = loads[8:]
    pl.semaphore_wait(barrier, SPANS + 1)

    def over_head(n, src, dst, to, first, count):
        at = pl.ds(first * PIECE, count * PIECE)
        return pltpu.make_async_remote_copy(
            src.at[:, at], dst.at[:, at], ag_send.at[n], ag_recv.at[n], device_id={"head": to}, device_id_type=MESH
        )

    first, second = range(4), range(4, 8)
    to_up = [over_head(n, go, gov.at[0], up, n, 1) for n in first]
    to_down = [over_head(n, go, gov.at[1], down, n, 1) for n in second]
    rest_up = over_head(8, go, gov.at[0], up, 4, 4)
    rest_down = over_head(9, go, gov.at[1], down, 0, 4)
    on_up = [over_head(10 + n, gov.at[0], gov.at[2], up, n, 1) for n in first]
    on_down = [over_head(10 + n, gov.at[1], gov.at[2], down, n, 1) for n in second]
    for n in first:
        to_up[n].start()
        to_down[n].start()

    flips = {0: x, 1: x + 1 - 2 * lax.rem(x, 2), 2: lax.rem(x + 2, 4), 3: 3 - x}
    turns = {0: z, 1: z + 1 - 2 * lax.rem(z, 2), 2: lax.rem(z + 2, 4), 3: 3 - z}
    hops = {0: 0, 1: 1, 2: 2, 3: 1}
    sides = []
    for side in ((2, 3), (1, 0)):
        steps = [(a, b, c) for a in side for b in range(4) for c in range(2) if a or b or c]
        steps.sort(key=lambda e: -hops[e[0]] - hops[e[1]])
        sides.append([flips[a] * 8 + turns[b] * 2 + (core if c == 0 else 1 - core) for a, b, c in steps])
    halves = (1 - x // 2, x // 2)

    def exchange(n, src, dst, to):
        return pltpu.make_async_remote_copy(
            src, dst, ex_send.at[n], ex_recv.at[n], device_id={"ctx": to}, device_id_type=MESH
        )

    def everything(n, src, dst):
        return exchange(n, src.at[pl.ds(0, SPANS - 1)], dst.at[pl.ds(0, SPANS - 1)], i)

    l_grp.wait()
    local = grp[...] - h * GROUPS
    before = jnp.where(iota((TOK, TOK), 0) < iota((TOK, TOK), 1), 1.0, 0.0).astype(BF16)
    names = iota((GROUPS, TOK), 0)
    total = jnp.zeros((GROUPS, 1), F32)
    for b in range(CH // TOK):
        row = local[b : b + 1, :]
        hot = jnp.where(names == row, 1.0, 0.0)
        count = jnp.sum(hot * (dot(hot.astype(BF16), before, 1, 0) + total), axis=0, keepdims=True)
        total = total + jnp.sum(hot, axis=1, keepdims=True)
        rank = (row & (OWN - 1)) * ROWS + lax.shift_right_logical(row, 1) * PER + count.astype(jnp.int32)
        for r in range(CH // TOK):
            perm[r * TOK : (r + 1) * TOK, b * TOK : (b + 1) * TOK] = jnp.where(
                iota((TOK, TOK), 0) + r * TOK == rank, 1.0, 0.0
            ).astype(BF16)

    l_q.wait()
    l_k.wait()
    gated = (qv[...].astype(F32) * kv[...].astype(F32)).astype(BF16)
    for u in range(OWN):
        gs[u] = dot(perm[u * ROWS : (u + 1) * ROWS, :], gated, 1, 1).astype(BF16).reshape(SPANS, PER, TOK)
    for side in sides:
        for to in side:
            exchange(0, gs.at[:, to], gr.at[:, i], to).start()
    gr[:, i] = gs[:, i]

    rest_up.start()
    rest_down.start()

    def features(block, slot, first=False):
        def tile(n, carry):
            at = pl.ds(pl.multiple_of(n * 256, 256), 256)
            part = dot(block[...], wv[slot, at, :], 1, 1)
            fg[:, at] = part if first else fg[:, at] + part
            return carry

        lax.fori_loop(0, CH // 256, tile, 0)

    l_own.wait()
    l_w[0].wait()
    features(own, 0, True)

    for n in first:
        to_up[n].wait_recv()
        on_up[n].start()
        to_down[n].wait_recv()
        on_down[n].start()

    l_doc.wait()
    block = lax.shift_right_logical(iota((ROWS, TOK), 0), 4)
    ends = [doc[0]]
    for n in range(1, 4):
        ends.append(ends[-1] + doc[n])
    end = jnp.where(block < ends[0], ends[0], jnp.where(block < ends[1], ends[1], jnp.where(block < ends[2], ends[2], ends[3])))
    rem[...] = (end - block).astype(F32).astype(BF16).reshape(SPANS, PER, TOK)
    xr[:, SPANS:] = jnp.zeros((OWN, LAGS - 1, PER, TOK), BF16)
    corr[:, KW:] = jnp.zeros((TOK, TOK), F32)

    l_filt.wait()
    for u in range(OWN):
        pick = jnp.where(iota((PER, GROUPS), 1) == i * OWN + u, 1.0, 0.0).astype(BF16)
        line = dot(pick, fv[...], 1, 0)
        line = jnp.concatenate([line, jnp.zeros((PER, TOK), F32)], axis=1)
        for c in range(TOK // PER):
            turned = pltpu.roll(line, c * PER, 1, stride=1, stride_axis=0)
            toep[u, c * PER : (c + 1) * PER, :] = turned[:, :KW].astype(BF16)

    rest_up.wait_recv()
    l_w[1].wait()
    features(gov.at[0], 1)
    rest_down.wait_recv()
    l_w[2].wait()
    features(gov.at[1], 2)

    exchange(0, gs.at[:, pl.ds(0, SPANS - 1)], gr.at[:, pl.ds(0, SPANS - 1)], i).wait_recv()
    flip = jnp.where(iota((TOK, TOK), 0) + iota((TOK, TOK), 1) == TOK - 1, 1.0, 0.0).astype(BF16)
    for u in range(OWN):
        for p, half in enumerate(halves):
            rows = gr[u, pl.ds(half * HALF, HALF)].reshape(ROWS // 2, TOK)
            gt[u, p] = dot(flip, rows, 1, 1).astype(BF16)

    l_w[3].wait()
    l_v.wait()
    far = gov.at[2]
    for n in first:
        on_up[n].wait_recv()
        on_down[n].wait_recv()
        one, two = pl.ds(n * PIECE, PIECE), pl.ds((4 + n) * PIECE, PIECE)
        rows = jnp.concatenate([far[:, one], far[:, two]], axis=1)
        for m in range(CH // 256):
            at = slice(m * 256, (m + 1) * 256)
            part = fg[:, at] + dot(rows, jnp.concatenate([wv[3, at, one], wv[3, at, two]], axis=1), 1, 1)
            if n < 3:
                fg[:, at] = part
            else:
                conv[:, at] = (part * vv[:, at].astype(F32)).astype(BF16)

    for u in range(OWN):
        for side, half in zip(sides, halves):
            at = pl.ds(pl.multiple_of(u * ROWS + half * (ROWS // 2), ROWS // 2), ROWS // 2)
            part = dot(perm[at, :], conv[...], 1, 1)
            xs[u, pl.ds(half * HALF, HALF)] = part.astype(BF16).reshape(HALF, PER, TOK)
            for to in side:
                exchange(1 + u, xs.at[u, to], xr.at[u, i], to).start()
        xr[u, i] = xs[u, i]

    for u in range(OWN):
        everything(1 + u, xs.at[u], xr.at[u]).wait_recv()
        for p, (side, half) in enumerate(zip(sides, halves)):
            left = rem[pl.ds(half * HALF, HALF)]
            acc = jnp.zeros((ROWS // 2, TOK), F32)
            for d in range(0, LAGS, 2):
                parts = [
                    jnp.where(left > e, xr[u, pl.ds(half * HALF + e, HALF)], jnp.zeros((), BF16)).reshape(ROWS // 2, TOK)
                    for e in range(d, min(d + 2, LAGS))
                ]
                at = slice(d * TOK, (d + len(parts)) * TOK)
                part = jnp.concatenate(parts, axis=1)
                amat[u, p, :, at] = part
                acc = acc + dot(part, toep[u, :, at], 1, 1)
            ys[u, pl.ds(half * HALF, HALF)] = acc.astype(BF16).reshape(HALF, PER, TOK)
            for to in side:
                exchange(3 + u, ys.at[u, to], yr.at[u, i], to).start()
        yr[u, i] = ys[u, i]

    for u in range(OWN):
        corr[:, :KW] = dot(gt[u, 0], amat[u, 0], 1, 0) + dot(gt[u, 1], amat[u, 1], 1, 0)
        acc = jnp.zeros((PER, KW + TOK), F32)
        for c in range(TOK // PER):
            acc = acc + pltpu.roll(corr[c * PER : (c + 1) * PER, :], 1 + c * PER, 1, stride=1, stride_axis=0)
        line = jnp.sum(acc, axis=0, keepdims=True)
        for d in range(LAGS):
            fs[d, u : u + 1, :] = line[:, (d + 1) * TOK : (d + 2) * TOK]
    for side in sides:
        for to in side:

            @pl.when(to < LAGS)
            def _(to=to):
                exchange(5, fs.at[to], fr.at[i], to).start()

    l_skip.wait()
    for u in range(OWN):
        everything(3 + u, ys.at[u], yr.at[u]).wait_recv()
        for n in range(CH // 256):
            at = slice(n * 256, (n + 1) * 256)
            part = dot(yr[u].reshape(ROWS, TOK), perm[u * ROWS : (u + 1) * ROWS, at], 0, 0)
            if u == 0:
                fg[:, at] = part + skip[:, at] * conv[:, at].astype(F32)
            else:
                grad = fg[:, at] + part
                out_q[:, at] = (grad * kv[:, at].astype(F32)).astype(BF16)
                out_k[:, at] = (grad * qv[:, at].astype(F32)).astype(BF16)

    @pl.when(i < LAGS)
    def _():
        fr[i] = fs[i]
        everything(5, fr, fr).wait_recv()
        exchange(5, fs.at[pl.ds(0, LAGS - 1)], fr.at[pl.ds(0, LAGS - 1)], i).wait_send()

    @pl.when(i >= LAGS)
    def _():
        fr[...] = jnp.zeros(fr.shape, F32)
        exchange(5, fs, fr.at[pl.ds(0, LAGS)], i).wait_send()

    for copy in (*to_up, *to_down, rest_up, rest_down, *on_up, *on_down):
        copy.wait_send()
    exchange(0, gs.at[:, pl.ds(0, SPANS - 1)], gr.at[:, pl.ds(0, SPANS - 1)], i).wait_send()
    for u in range(OWN):
        everything(1 + u, xs.at[u], xr.at[u]).wait_send()
        everything(3 + u, ys.at[u], yr.at[u]).wait_send()


def finish(out_q, out_k, fr, gq, gk, gf, out_f, sem):
    copies = [pltpu.make_async_copy(src, dst, sem.at[n]) for n, (src, dst) in enumerate(((out_q, gq), (out_k, gk), (out_f, gf)))]
    copies[0].start()
    copies[1].start()
    for t in range(SPANS):
        out_f[t * OWN : (t + 1) * OWN, :] = fr[t]
    copies[2].start()
    for copy in copies:
        copy.wait()


def per_device(
    query_proj, key_proj, value_proj, grad_out, out_proj, filters, skip_gain, doc_lengths, group_of
):
    hbm = pl.BlockSpec(memory_space=pltpu.HBM)
    vmem = pl.BlockSpec(memory_space=pltpu.VMEM)
    dma = pltpu.SemaphoreType.DMA
    blocks = (OWN, SPANS, PER, TOK)
    rows = (TOK, CH)
    args = (
        doc_lengths, grad_out, query_proj, key_proj, value_proj, out_proj, filters,
        group_of.reshape(CH // TOK, TOK), skip_gain.reshape(1, CH),
    )
    held = pl.pallas_call(
        kernel,
        out_shape=(
            jax.ShapeDtypeStruct(rows, BF16),
            jax.ShapeDtypeStruct(rows, BF16),
            jax.ShapeDtypeStruct((SPANS, OWN, TOK), F32),
        ),
        in_specs=[hbm] * 9,
        out_specs=(vmem,) * 3,
        scratch_shapes=[
            pltpu.VMEM(blocks, BF16),
            pltpu.VMEM((CH, CH), BF16),
            pltpu.VMEM(rows, BF16),
            pltpu.VMEM(rows, BF16),
            pltpu.VMEM(rows, BF16),
            pltpu.VMEM((1, CH), F32),
            pltpu.VMEM(rows, BF16),
            pltpu.VMEM((HEADS - 1, *rows), BF16),
            pltpu.VMEM(rows, BF16),
            pltpu.VMEM((HEADS, CH, CH), BF16),
            pltpu.VMEM((GROUPS, KW), BF16),
            pltpu.VMEM((CH // TOK, TOK), jnp.int32),
            pltpu.SMEM((4,), jnp.int32),
            pltpu.VMEM(rows, F32),
            pltpu.VMEM((SPANS, PER, TOK), BF16),
            pltpu.VMEM(blocks, BF16),
            pltpu.VMEM(blocks, BF16),
            pltpu.VMEM(blocks, BF16),
            pltpu.VMEM((OWN, SPANS + LAGS - 1, PER, TOK), BF16),
            pltpu.VMEM(blocks, BF16),
            pltpu.VMEM((OWN, TOK, KW), BF16),
            pltpu.VMEM((OWN, 2, ROWS // 2, KW), BF16),
            pltpu.VMEM((OWN, 2, TOK, ROWS // 2), BF16),
            pltpu.VMEM((TOK, KW + TOK), F32),
            pltpu.VMEM((LAGS, OWN, TOK), F32),
            dma((12,)),
            dma((18,)),
            dma((18,)),
            dma((6,)),
            dma((6,)),
        ],
        compiler_params=pltpu.CompilerParams(
            collective_id=0, has_side_effects=True, vmem_limit_bytes=40 << 20
        ),
    )(*(pltpu.with_memory_space_constraint(arg, pltpu.HBM) for arg in args))
    return pl.pallas_call(
        finish,
        out_shape=(
            jax.ShapeDtypeStruct(rows, BF16),
            jax.ShapeDtypeStruct(rows, BF16),
            jax.ShapeDtypeStruct((GROUPS, TOK), F32),
        ),
        in_specs=[vmem] * 3,
        out_specs=(hbm,) * 3,
        scratch_shapes=[pltpu.VMEM((GROUPS, TOK), F32), dma((3,))],
        compiler_params=pltpu.CompilerParams(vmem_limit_bytes=16 << 20),
    )(*held)


def solution(mesh):
    in_specs = (
        P("ctx", "head"),
        P("ctx", "head"),
        P("ctx", "head"),
        P("ctx", "head"),
        P("head", None),
        P("head", None),
        P("head"),
        P(),
        P("head"),
    )
    out_specs = (P("ctx", "head"), P("ctx", "head"), P("head", "ctx"))
    return jax.shard_map(
        per_device, mesh=mesh, in_specs=in_specs, out_specs=out_specs, check_vma=False
    )
```

```python
import jax
import jax.numpy as jnp
from jax import lax
from jax.experimental import pallas as pl
from jax.experimental.pallas import tpu as pltpu
from jax.sharding import PartitionSpec as P

TOK = 128
SPANS = 32
HEADS = 4
CH = 1024
GROUPS = 64
PER = 16
OWN = GROUPS // SPANS
LAGS = 17
KW = LAGS * TOK
HALF = SPANS // 2
PIECE = CH // 8
ROWS = SPANS * PER
MESH = pl.DeviceIdType.MESH
F32 = jnp.float32
BF16 = jnp.bfloat16


def dot(a, b, ca, cb):
    return lax.dot_general(a, b, (((ca,), (cb,)), ((), ())), preferred_element_type=F32)


def iota(shape, dim):
    return lax.broadcasted_iota(jnp.int32, shape, dim)


def kernel(
    doc_in, go, q, k, v, w, filt, grp_in, skip_in,
    out_q, out_k, fr,
    yr, perm, conv, qv, kv, skip, own, gov, vv, wv, fv, grp, doc, fg, rem, gs, gr, xs, xr, ys, toep, amat, gt, corr, fs,
    loc, ag_send, ag_recv, ex_send, ex_recv,
):
    i = lax.axis_index("ctx")
    h = lax.axis_index("head")
    up = lax.rem(h + 1, HEADS)
    down = lax.rem(h + HEADS - 1, HEADS)
    across = lax.rem(h + 2, HEADS)
    x, z, core = i // 8, lax.rem(i // 2, 4), lax.rem(i, 2)

    barrier = pltpu.get_barrier_semaphore()
    pl.semaphore_signal(barrier, inc=1, device_id={"head": up}, device_id_type=MESH)
    pl.semaphore_signal(barrier, inc=1, device_id={"head": down}, device_id_type=MESH)

    def greet(n, carry):
        pl.semaphore_signal(barrier, inc=1, device_id={"ctx": lax.rem(i + n, SPANS)}, device_id_type=MESH)
        return carry

    lax.fori_loop(1, SPANS, greet, 0)

    pairs = [(grp_in, grp), (go, own), (q, qv), (k, kv), (doc_in, doc), (filt.at[:, pl.ds(0, KW)], fv), (v, vv), (skip_in, skip)]
    for slot, block in enumerate((h, down, up, across)):
        pairs.append((w.at[:, pl.ds(pl.multiple_of(block * CH, CH), CH)], wv.at[slot]))
    loads = [pltpu.make_async_copy(src, dst, loc.at[n]) for n, (src, dst) in enumerate(pairs)]
    for load in loads:
        load.start()
    l_grp, l_own, l_q, l_k, l_doc, l_filt, l_v, l_skip = loads[:8]
    l_w = loads[8:]
    pl.semaphore_wait(barrier, SPANS + 1)

    def over_head(n, src, dst, to, first, count):
        at = pl.ds(first * PIECE, count * PIECE)
        return pltpu.make_async_remote_copy(
            src.at[:, at], dst.at[:, at], ag_send.at[n], ag_recv.at[n], device_id={"head": to}, device_id_type=MESH
        )

    first, second = range(4), range(4, 8)
    to_up = [over_head(n, own, gov.at[0], up, n, 1) for n in first]
    to_down = [over_head(n, own, gov.at[1], down, n, 1) for n in second]
    rest_up = over_head(8, own, gov.at[0], up, 4, 4)
    rest_down = over_head(9, own, gov.at[1], down, 0, 4)
    on_up = [over_head(10 + n, gov.at[0], gov.at[2], up, n, 1) for n in first]
    on_down = [over_head(10 + n, gov.at[1], gov.at[2], down, n, 1) for n in second]
    l_own.wait()
    for n in first:
        to_up[n].start()
        to_down[n].start()

    flips = {0: x, 1: x + 1 - 2 * lax.rem(x, 2), 2: lax.rem(x + 2, 4), 3: 3 - x}
    turns = {0: z, 1: z + 1 - 2 * lax.rem(z, 2), 2: lax.rem(z + 2, 4), 3: 3 - z}
    hops = {0: 0, 1: 1, 2: 2, 3: 1}

    def by_distance(steps):
        steps = sorted(steps, key=lambda e: -hops[e[0]] - hops[e[1]])
        return [flips[a] * 8 + turns[b] * 2 + (core if c == 0 else 1 - core) for a, b, c in steps]

    halves = (1 - x // 2, x // 2)
    steps = [(a, b, c) for a in range(4) for b in range(4) for c in range(2) if a or b or c]
    partners = by_distance(steps)
    sides = [by_distance([e for e in steps if (e[0] > 1) == far]) for far in (True, False)]

    def exchange(n, src, dst, to):
        return pltpu.make_async_remote_copy(
            src, dst, ex_send.at[n], ex_recv.at[n], device_id={"ctx": to}, device_id_type=MESH
        )

    def both(n, src, dst):
        return exchange(n, src.at[:, pl.ds(0, SPANS - 1)], dst.at[:, pl.ds(0, SPANS - 1)], i)

    l_grp.wait()
    local = grp[...] - h * GROUPS
    before = jnp.where(iota((TOK, TOK), 0) < iota((TOK, TOK), 1), 1.0, 0.0).astype(BF16)
    names = iota((GROUPS, TOK), 0)
    total = jnp.zeros((GROUPS, 1), F32)
    for b in range(CH // TOK):
        row = local[b : b + 1, :]
        hot = jnp.where(names == row, 1.0, 0.0)
        count = jnp.sum(hot * (dot(hot.astype(BF16), before, 1, 0) + total), axis=0, keepdims=True)
        total = total + jnp.sum(hot, axis=1, keepdims=True)
        rank = (row & (OWN - 1)) * ROWS + lax.shift_right_logical(row, 1) * PER + count.astype(jnp.int32)
        for r in range(CH // TOK):
            perm[r * TOK : (r + 1) * TOK, b * TOK : (b + 1) * TOK] = jnp.where(
                iota((TOK, TOK), 0) + r * TOK == rank, 1.0, 0.0
            ).astype(BF16)

    l_q.wait()
    l_k.wait()
    gated = (qv[...].astype(F32) * kv[...].astype(F32)).astype(BF16)
    for u in range(OWN):
        gs[u] = dot(perm[u * ROWS : (u + 1) * ROWS, :], gated, 1, 1).astype(BF16).reshape(SPANS, PER, TOK)
    for to in partners:
        exchange(0, gs.at[:, to], gr.at[:, i], to).start()
    gr[:, i] = gs[:, i]

    rest_up.start()
    rest_down.start()

    def features(block, slot, first=False):
        def tile(n, carry):
            at = pl.ds(pl.multiple_of(n * 256, 256), 256)
            part = dot(block[...], wv[slot, at, :], 1, 1)
            fg[:, at] = part if first else fg[:, at] + part
            return carry

        lax.fori_loop(0, CH // 256, tile, 0)

    l_w[0].wait()
    features(own, 0, True)

    for n in first:
        to_up[n].wait_recv()
        on_up[n].start()
        to_down[n].wait_recv()
        on_down[n].start()

    l_doc.wait()
    block = lax.shift_right_logical(iota((ROWS, TOK), 0), 4)
    ends = [doc[0]]
    for n in range(1, 4):
        ends.append(ends[-1] + doc[n])
    end = jnp.where(block < ends[0], ends[0], jnp.where(block < ends[1], ends[1], jnp.where(block < ends[2], ends[2], ends[3])))
    rem[...] = (end - block).astype(F32).astype(BF16).reshape(SPANS, PER, TOK)
    xr[:, SPANS:] = jnp.zeros((OWN, LAGS - 1, PER, TOK), BF16)
    corr[:, KW:] = jnp.zeros((TOK, TOK), F32)

    l_filt.wait()
    for u in range(OWN):
        pick = jnp.where(iota((PER, GROUPS), 1) == i * OWN + u, 1.0, 0.0).astype(BF16)
        line = dot(pick, fv[...], 1, 0)
        line = jnp.concatenate([line, jnp.zeros((PER, TOK), F32)], axis=1)
        for c in range(TOK // PER):
            turned = pltpu.roll(line, c * PER, 1, stride=1, stride_axis=0)
            toep[u, c * PER : (c + 1) * PER, :] = turned[:, :KW].astype(BF16)

    rest_up.wait_recv()
    l_w[1].wait()
    features(gov.at[0], 1)
    rest_down.wait_recv()
    l_w[2].wait()
    features(gov.at[1], 2)

    both(0, gs, gr).wait_recv()
    flip = jnp.where(iota((TOK, TOK), 0) + iota((TOK, TOK), 1) == TOK - 1, 1.0, 0.0).astype(BF16)
    for u in range(OWN):
        for p, half in enumerate(halves):
            rows = gr[u, pl.ds(half * HALF, HALF)].reshape(ROWS // 2, TOK)
            gt[u, p] = dot(flip, rows, 1, 1).astype(BF16)

    l_w[3].wait()
    l_v.wait()
    far = gov.at[2]
    for n in first:
        on_up[n].wait_recv()
        on_down[n].wait_recv()
        one, two = pl.ds(n * PIECE, PIECE), pl.ds((4 + n) * PIECE, PIECE)
        rows = jnp.concatenate([far[:, one], far[:, two]], axis=1)
        for m in range(CH // 256):
            at = slice(m * 256, (m + 1) * 256)
            part = fg[:, at] + dot(rows, jnp.concatenate([wv[3, at, one], wv[3, at, two]], axis=1), 1, 1)
            if n < 3:
                fg[:, at] = part
            else:
                conv[:, at] = (part * vv[:, at].astype(F32)).astype(BF16)

    for u in range(OWN):
        part = dot(perm[u * ROWS : (u + 1) * ROWS, :], conv[...], 1, 1)
        xs[u] = part.astype(BF16).reshape(SPANS, PER, TOK)
    for to in partners:
        exchange(1, xs.at[:, to], xr.at[:, i], to).start()
    xr[:, i] = xs[:, i]

    both(1, xs, xr).wait_recv()
    for p, (side, half) in enumerate(zip(sides, halves)):
        left = rem[pl.ds(half * HALF, HALF)]
        for u in range(OWN):
            acc = jnp.zeros((ROWS // 2, TOK), F32)
            for d in range(0, LAGS, 2):
                parts = [
                    jnp.where(left > e, xr[u, pl.ds(half * HALF + e, HALF)], jnp.zeros((), BF16)).reshape(ROWS // 2, TOK)
                    for e in range(d, min(d + 2, LAGS))
                ]
                at = slice(d * TOK, (d + len(parts)) * TOK)
                part = jnp.concatenate(parts, axis=1)
                amat[u, p, :, at] = part
                acc = acc + dot(part, toep[u, :, at], 1, 1)
            ys[u, pl.ds(half * HALF, HALF)] = acc.astype(BF16).reshape(HALF, PER, TOK)
        for to in side:
            exchange(2, ys.at[:, to], yr.at[:, i], to).start()
    yr[:, i] = ys[:, i]

    for u in range(OWN):
        corr[:, :KW] = dot(gt[u, 0], amat[u, 0], 1, 0) + dot(gt[u, 1], amat[u, 1], 1, 0)
        acc = jnp.zeros((PER, KW + TOK), F32)
        for c in range(TOK // PER):
            acc = acc + pltpu.roll(corr[c * PER : (c + 1) * PER, :], 1 + c * PER, 1, stride=1, stride_axis=0)
        line = jnp.sum(acc, axis=0, keepdims=True)
        for d in range(LAGS):
            fs[d, u : u + 1, :] = line[:, (d + 1) * TOK : (d + 2) * TOK]
    for side in sides:
        for to in side:

            @pl.when(to < LAGS)
            def _(to=to):
                exchange(3, fs.at[to], fr.at[i], to).start()

    l_skip.wait()
    both(2, ys, yr).wait_recv()
    for u in range(OWN):
        for n in range(CH // 256):
            at = slice(n * 256, (n + 1) * 256)
            part = dot(yr[u].reshape(ROWS, TOK), perm[u * ROWS : (u + 1) * ROWS, at], 0, 0)
            if u == 0:
                fg[:, at] = part + skip[:, at] * conv[:, at].astype(F32)
            else:
                grad = fg[:, at] + part
                out_q[:, at] = (grad * kv[:, at].astype(F32)).astype(BF16)
                out_k[:, at] = (grad * qv[:, at].astype(F32)).astype(BF16)

    @pl.when(i < LAGS)
    def _():
        fr[i] = fs[i]
        exchange(3, fr.at[pl.ds(0, SPANS - 1)], fr.at[pl.ds(0, SPANS - 1)], i).wait_recv()
        exchange(3, fs.at[pl.ds(0, LAGS - 1)], fr.at[pl.ds(0, LAGS - 1)], i).wait_send()

    @pl.when(i >= LAGS)
    def _():
        fr[...] = jnp.zeros(fr.shape, F32)
        exchange(3, fs, fr.at[pl.ds(0, LAGS)], i).wait_send()

    for copy in (*to_up, *to_down, rest_up, rest_down, *on_up, *on_down):
        copy.wait_send()
    both(0, gs, gr).wait_send()
    both(1, xs, xr).wait_send()
    both(2, ys, yr).wait_send()


def finish(out_q, out_k, fr, gq, gk, gf, out_f, sem):
    copies = [pltpu.make_async_copy(src, dst, sem.at[n]) for n, (src, dst) in enumerate(((out_q, gq), (out_k, gk), (out_f, gf)))]
    copies[0].start()
    copies[1].start()
    for t in range(SPANS):
        out_f[t * OWN : (t + 1) * OWN, :] = fr[t]
    copies[2].start()
    for copy in copies:
        copy.wait()


def per_device(
    query_proj, key_proj, value_proj, grad_out, out_proj, filters, skip_gain, doc_lengths, group_of
):
    hbm = pl.BlockSpec(memory_space=pltpu.HBM)
    vmem = pl.BlockSpec(memory_space=pltpu.VMEM)
    dma = pltpu.SemaphoreType.DMA
    blocks = (OWN, SPANS, PER, TOK)
    rows = (TOK, CH)
    args = (
        doc_lengths, grad_out, query_proj, key_proj, value_proj, out_proj, filters,
        group_of.reshape(CH // TOK, TOK), skip_gain.reshape(1, CH),
    )
    held = pl.pallas_call(
        kernel,
        out_shape=(
            jax.ShapeDtypeStruct(rows, BF16),
            jax.ShapeDtypeStruct(rows, BF16),
            jax.ShapeDtypeStruct((SPANS, OWN, TOK), F32),
        ),
        in_specs=[hbm] * 9,
        out_specs=(vmem,) * 3,
        scratch_shapes=[
            pltpu.VMEM(blocks, BF16),
            pltpu.VMEM((CH, CH), BF16),
            pltpu.VMEM(rows, BF16),
            pltpu.VMEM(rows, BF16),
            pltpu.VMEM(rows, BF16),
            pltpu.VMEM((1, CH), F32),
            pltpu.VMEM(rows, BF16),
            pltpu.VMEM((HEADS - 1, *rows), BF16),
            pltpu.VMEM(rows, BF16),
            pltpu.VMEM((HEADS, CH, CH), BF16),
            pltpu.VMEM((GROUPS, KW), BF16),
            pltpu.VMEM((CH // TOK, TOK), jnp.int32),
            pltpu.SMEM((4,), jnp.int32),
            pltpu.VMEM(rows, F32),
            pltpu.VMEM((SPANS, PER, TOK), BF16),
            pltpu.VMEM(blocks, BF16),
            pltpu.VMEM(blocks, BF16),
            pltpu.VMEM(blocks, BF16),
            pltpu.VMEM((OWN, SPANS + LAGS - 1, PER, TOK), BF16),
            pltpu.VMEM(blocks, BF16),
            pltpu.VMEM((OWN, TOK, KW), BF16),
            pltpu.VMEM((OWN, 2, ROWS // 2, KW), BF16),
            pltpu.VMEM((OWN, 2, TOK, ROWS // 2), BF16),
            pltpu.VMEM((TOK, KW + TOK), F32),
            pltpu.VMEM((LAGS, OWN, TOK), F32),
            dma((12,)),
            dma((18,)),
            dma((18,)),
            dma((4,)),
            dma((4,)),
        ],
        compiler_params=pltpu.CompilerParams(
            collective_id=0, has_side_effects=True, vmem_limit_bytes=40 << 20
        ),
    )(*(pltpu.with_memory_space_constraint(arg, pltpu.HBM) for arg in args))
    return pl.pallas_call(
        finish,
        out_shape=(
            jax.ShapeDtypeStruct(rows, BF16),
            jax.ShapeDtypeStruct(rows, BF16),
            jax.ShapeDtypeStruct((GROUPS, TOK), F32),
        ),
        in_specs=[vmem] * 3,
        out_specs=(hbm,) * 3,
        scratch_shapes=[pltpu.VMEM((GROUPS, TOK), F32), dma((3,))],
        compiler_params=pltpu.CompilerParams(vmem_limit_bytes=16 << 20),
    )(*held)


def solution(mesh):
    in_specs = (
        P("ctx", "head"),
        P("ctx", "head"),
        P("ctx", "head"),
        P("ctx", "head"),
        P("head", None),
        P("head", None),
        P("head"),
        P(),
        P("head"),
    )
    out_specs = (P("ctx", "head"), P("ctx", "head"), P("head", "ctx"))
    return jax.shard_map(
        per_device, mesh=mesh, in_specs=in_specs, out_specs=out_specs, check_vma=False
    )
```

```python
import jax
import jax.numpy as jnp
from jax import lax
from jax.experimental import pallas as pl
from jax.experimental.pallas import tpu as pltpu
from jax.sharding import PartitionSpec as P

TOK = 128
SPANS = 32
HEADS = 4
CH = 1024
GROUPS = 64
PER = 16
OWN = GROUPS // SPANS
LAGS = 17
KW = LAGS * TOK
HALF = SPANS // 2
PIECE = CH // 8
ROWS = SPANS * PER
MESH = pl.DeviceIdType.MESH
F32 = jnp.float32
BF16 = jnp.bfloat16


def dot(a, b, ca, cb):
    return lax.dot_general(a, b, (((ca,), (cb,)), ((), ())), preferred_element_type=F32)


def iota(shape, dim):
    return lax.broadcasted_iota(jnp.int32, shape, dim)


def kernel(
    doc_in, go, q, k, v, w, filt, grp_in, skip_in,
    out_q, out_k, fr,
    yr, perm, conv, qv, kv, skip, own, gov, vv, wv, fv, grp, doc, fg, rem, gs, gr, xs, xr, ys, toep, amat, gt, corr, fs, gain,
    loc, ag_send, ag_recv, ex_send, ex_recv,
):
    i = lax.axis_index("ctx")
    h = lax.axis_index("head")
    up = lax.rem(h + 1, HEADS)
    down = lax.rem(h + HEADS - 1, HEADS)
    across = lax.rem(h + 2, HEADS)
    x, z, core = i // 8, lax.rem(i // 2, 4), lax.rem(i, 2)

    barrier = pltpu.get_barrier_semaphore()
    pl.semaphore_signal(barrier, inc=1, device_id={"head": up}, device_id_type=MESH)
    pl.semaphore_signal(barrier, inc=1, device_id={"head": down}, device_id_type=MESH)

    def greet(n, carry):
        pl.semaphore_signal(barrier, inc=1, device_id={"ctx": lax.rem(i + n, SPANS)}, device_id_type=MESH)
        return carry

    lax.fori_loop(1, SPANS, greet, 0)

    pairs = [(grp_in, grp), (go, own), (q, qv), (k, kv), (doc_in, doc), (filt.at[:, pl.ds(0, KW)], fv), (v, vv), (skip_in, skip)]
    for slot, block in enumerate((h, down, up, across)):
        pairs.append((w.at[:, pl.ds(pl.multiple_of(block * CH, CH), CH)], wv.at[slot]))
    loads = [pltpu.make_async_copy(src, dst, loc.at[n]) for n, (src, dst) in enumerate(pairs)]
    for load in loads:
        load.start()
    l_grp, l_own, l_q, l_k, l_doc, l_filt, l_v, l_skip = loads[:8]
    l_w = loads[8:]
    pl.semaphore_wait(barrier, SPANS + 1)

    def over_head(n, src, dst, to, first, count):
        at = pl.ds(first * PIECE, count * PIECE)
        return pltpu.make_async_remote_copy(
            src.at[:, at], dst.at[:, at], ag_send.at[n], ag_recv.at[n], device_id={"head": to}, device_id_type=MESH
        )

    first, second = range(4), range(4, 8)
    to_up = [over_head(n, own, gov.at[0], up, n, 1) for n in first]
    to_down = [over_head(n, own, gov.at[1], down, n, 1) for n in second]
    rest_up = over_head(8, own, gov.at[0], up, 4, 4)
    rest_down = over_head(9, own, gov.at[1], down, 0, 4)
    on_up = [over_head(10 + n, gov.at[0], gov.at[2], up, n, 1) for n in first]
    on_down = [over_head(10 + n, gov.at[1], gov.at[2], down, n, 1) for n in second]
    l_own.wait()
    for n in first:
        to_up[n].start()
        to_down[n].start()

    flips = {0: x, 1: x + 1 - 2 * lax.rem(x, 2), 2: lax.rem(x + 2, 4), 3: 3 - x}
    turns = {0: z, 1: z + 1 - 2 * lax.rem(z, 2), 2: lax.rem(z + 2, 4), 3: 3 - z}
    hops = {0: 0, 1: 1, 2: 2, 3: 1}

    def by_distance(steps):
        steps = sorted(steps, key=lambda e: -hops[e[0]] - hops[e[1]])
        return [flips[a] * 8 + turns[b] * 2 + (core if c == 0 else 1 - core) for a, b, c in steps]

    halves = (1 - x // 2, x // 2)
    steps = [(a, b, c) for a in range(4) for b in range(4) for c in range(2) if a or b or c]
    partners = by_distance(steps)
    sides = [by_distance([e for e in steps if (e[0] > 1) == far]) for far in (True, False)]

    def exchange(n, src, dst, to):
        return pltpu.make_async_remote_copy(
            src, dst, ex_send.at[n], ex_recv.at[n], device_id={"ctx": to}, device_id_type=MESH
        )

    def both(n, src, dst):
        return exchange(n, src.at[:, pl.ds(0, SPANS - 1)], dst.at[:, pl.ds(0, SPANS - 1)], i)

    l_grp.wait()
    local = grp[...] - h * GROUPS
    before = jnp.where(iota((TOK, TOK), 0) < iota((TOK, TOK), 1), 1.0, 0.0).astype(BF16)
    names = iota((GROUPS, TOK), 0)
    total = jnp.zeros((GROUPS, 1), F32)
    for b in range(CH // TOK):
        row = local[b : b + 1, :]
        hot = jnp.where(names == row, 1.0, 0.0)
        count = jnp.sum(hot * (dot(hot.astype(BF16), before, 1, 0) + total), axis=0, keepdims=True)
        total = total + jnp.sum(hot, axis=1, keepdims=True)
        rank = (row & (OWN - 1)) * ROWS + lax.shift_right_logical(row, 1) * PER + count.astype(jnp.int32)
        for r in range(CH // TOK):
            perm[r * TOK : (r + 1) * TOK, b * TOK : (b + 1) * TOK] = jnp.where(
                iota((TOK, TOK), 0) + r * TOK == rank, 1.0, 0.0
            ).astype(BF16)

    l_q.wait()
    l_k.wait()
    gated = (qv[...].astype(F32) * kv[...].astype(F32)).astype(BF16)
    for u in range(OWN):
        gs[u] = dot(perm[u * ROWS : (u + 1) * ROWS, :], gated, 1, 1).astype(BF16).reshape(SPANS, PER, TOK)
    for to in partners:
        exchange(0, gs.at[:, to], gr.at[:, i], to).start()
    gr[:, i] = gs[:, i]

    rest_up.start()
    rest_down.start()

    def features(block, slot, first=False):
        def tile(n, carry):
            at = pl.ds(pl.multiple_of(n * 256, 256), 256)
            part = dot(block[...], wv[slot, at, :], 1, 1)
            fg[:, at] = part if first else fg[:, at] + part
            return carry

        lax.fori_loop(0, CH // 256, tile, 0)

    l_w[0].wait()
    features(own, 0, True)

    for n in first:
        to_up[n].wait_recv()
        on_up[n].start()
        to_down[n].wait_recv()
        on_down[n].start()

    l_doc.wait()
    block = lax.shift_right_logical(iota((ROWS, TOK), 0), 4)
    ends = [doc[0]]
    for n in range(1, 4):
        ends.append(ends[-1] + doc[n])
    end = jnp.where(block < ends[0], ends[0], jnp.where(block < ends[1], ends[1], jnp.where(block < ends[2], ends[2], ends[3])))
    rem[...] = (end - block).astype(F32).astype(BF16).reshape(SPANS, PER, TOK)
    xr[:, SPANS:] = jnp.zeros((OWN, LAGS - 1, PER, TOK), BF16)
    corr[:, KW:] = jnp.zeros((TOK, TOK), F32)

    l_skip.wait()
    for u in range(OWN):
        hot = perm[pl.ds(pl.multiple_of(u * ROWS + i * PER, PER), PER), :].astype(F32)
        gain[u] = jnp.broadcast_to(jnp.sum(hot * skip[...], axis=1, keepdims=True), (PER, TOK))

    l_filt.wait()
    for u in range(OWN):
        pick = jnp.where(iota((PER, GROUPS), 1) == i * OWN + u, 1.0, 0.0).astype(BF16)
        line = dot(pick, fv[...], 1, 0)
        line = jnp.concatenate([line, jnp.zeros((PER, TOK), F32)], axis=1)
        for c in range(TOK // PER):
            turned = pltpu.roll(line, c * PER, 1, stride=1, stride_axis=0)
            toep[u, c * PER : (c + 1) * PER, :] = turned[:, :KW].astype(BF16)

    rest_up.wait_recv()
    l_w[1].wait()
    features(gov.at[0], 1)
    rest_down.wait_recv()
    l_w[2].wait()
    features(gov.at[1], 2)

    both(0, gs, gr).wait_recv()
    flip = jnp.where(iota((TOK, TOK), 0) + iota((TOK, TOK), 1) == TOK - 1, 1.0, 0.0).astype(BF16)
    for u in range(OWN):
        for p, half in enumerate(halves):
            rows = gr[u, pl.ds(half * HALF, HALF)].reshape(ROWS // 2, TOK)
            gt[u, p] = dot(flip, rows, 1, 1).astype(BF16)

    l_w[3].wait()
    l_v.wait()
    far = gov.at[2]
    for n in first:
        on_up[n].wait_recv()
        on_down[n].wait_recv()
        one, two = pl.ds(n * PIECE, PIECE), pl.ds((4 + n) * PIECE, PIECE)
        rows = jnp.concatenate([far[:, one], far[:, two]], axis=1)
        for m in range(CH // 256):
            at = slice(m * 256, (m + 1) * 256)
            part = fg[:, at] + dot(rows, jnp.concatenate([wv[3, at, one], wv[3, at, two]], axis=1), 1, 1)
            if n < 3:
                fg[:, at] = part
            else:
                conv[:, at] = (part * vv[:, at].astype(F32)).astype(BF16)

    for u in range(OWN):
        part = dot(perm[u * ROWS : (u + 1) * ROWS, :], conv[...], 1, 1)
        xs[u] = part.astype(BF16).reshape(SPANS, PER, TOK)
    for to in partners:
        exchange(1, xs.at[:, to], xr.at[:, i], to).start()
    xr[:, i] = xs[:, i]

    both(1, xs, xr).wait_recv()
    for p, (side, half) in enumerate(zip(sides, halves)):
        left = rem[pl.ds(half * HALF, HALF)]
        for u in range(OWN):
            acc = (xr[u, pl.ds(half * HALF, HALF)].astype(F32) * gain[u][None]).reshape(ROWS // 2, TOK)
            for d in range(0, LAGS, 2):
                parts = [
                    jnp.where(left > e, xr[u, pl.ds(half * HALF + e, HALF)], jnp.zeros((), BF16)).reshape(ROWS // 2, TOK)
                    for e in range(d, min(d + 2, LAGS))
                ]
                at = slice(d * TOK, (d + len(parts)) * TOK)
                part = jnp.concatenate(parts, axis=1)
                amat[u, p, :, at] = part
                acc = acc + dot(part, toep[u, :, at], 1, 1)
            ys[u, pl.ds(half * HALF, HALF)] = acc.astype(BF16).reshape(HALF, PER, TOK)
        for to in side:
            exchange(2, ys.at[:, to], yr.at[:, i], to).start()
    yr[:, i] = ys[:, i]

    for u in range(OWN):
        corr[:, :KW] = dot(gt[u, 0], amat[u, 0], 1, 0) + dot(gt[u, 1], amat[u, 1], 1, 0)
        acc = jnp.zeros((PER, KW + TOK), F32)
        for c in range(TOK // PER):
            acc = acc + pltpu.roll(corr[c * PER : (c + 1) * PER, :], 1 + c * PER, 1, stride=1, stride_axis=0)
        line = jnp.sum(acc, axis=0, keepdims=True)
        for d in range(LAGS):
            fs[d, u : u + 1, :] = line[:, (d + 1) * TOK : (d + 2) * TOK]
    for side in sides:
        for to in side:

            @pl.when(to < LAGS)
            def _(to=to):
                exchange(3, fs.at[to], fr.at[i], to).start()

    both(2, ys, yr).wait_recv()
    for u in range(OWN):
        for n in range(CH // 256):
            at = slice(n * 256, (n + 1) * 256)
            part = dot(yr[u].reshape(ROWS, TOK), perm[u * ROWS : (u + 1) * ROWS, at], 0, 0)
            if u == 0:
                fg[:, at] = part
            else:
                grad = fg[:, at] + part
                out_q[:, at] = (grad * kv[:, at].astype(F32)).astype(BF16)
                out_k[:, at] = (grad * qv[:, at].astype(F32)).astype(BF16)

    @pl.when(i < LAGS)
    def _():
        fr[i] = fs[i]
        exchange(3, fr.at[pl.ds(0, SPANS - 1)], fr.at[pl.ds(0, SPANS - 1)], i).wait_recv()
        exchange(3, fs.at[pl.ds(0, LAGS - 1)], fr.at[pl.ds(0, LAGS - 1)], i).wait_send()

    @pl.when(i >= LAGS)
    def _():
        fr[...] = jnp.zeros(fr.shape, F32)
        exchange(3, fs, fr.at[pl.ds(0, LAGS)], i).wait_send()

    for copy in (*to_up, *to_down, rest_up, rest_down, *on_up, *on_down):
        copy.wait_send()
    both(0, gs, gr).wait_send()
    both(1, xs, xr).wait_send()
    both(2, ys, yr).wait_send()


def finish(out_q, out_k, fr, gq, gk, gf, out_f, sem):
    copies = [pltpu.make_async_copy(src, dst, sem.at[n]) for n, (src, dst) in enumerate(((out_q, gq), (out_k, gk), (out_f, gf)))]
    copies[0].start()
    copies[1].start()
    for t in range(SPANS):
        out_f[t * OWN : (t + 1) * OWN, :] = fr[t]
    copies[2].start()
    for copy in copies:
        copy.wait()


def per_device(
    query_proj, key_proj, value_proj, grad_out, out_proj, filters, skip_gain, doc_lengths, group_of
):
    hbm = pl.BlockSpec(memory_space=pltpu.HBM)
    vmem = pl.BlockSpec(memory_space=pltpu.VMEM)
    dma = pltpu.SemaphoreType.DMA
    blocks = (OWN, SPANS, PER, TOK)
    rows = (TOK, CH)
    args = (
        doc_lengths, grad_out, query_proj, key_proj, value_proj, out_proj, filters,
        group_of.reshape(CH // TOK, TOK), skip_gain.reshape(1, CH),
    )
    held = pl.pallas_call(
        kernel,
        out_shape=(
            jax.ShapeDtypeStruct(rows, BF16),
            jax.ShapeDtypeStruct(rows, BF16),
            jax.ShapeDtypeStruct((SPANS, OWN, TOK), F32),
        ),
        in_specs=[hbm] * 9,
        out_specs=(vmem,) * 3,
        scratch_shapes=[
            pltpu.VMEM(blocks, BF16),
            pltpu.VMEM((CH, CH), BF16),
            pltpu.VMEM(rows, BF16),
            pltpu.VMEM(rows, BF16),
            pltpu.VMEM(rows, BF16),
            pltpu.VMEM((1, CH), F32),
            pltpu.VMEM(rows, BF16),
            pltpu.VMEM((HEADS - 1, *rows), BF16),
            pltpu.VMEM(rows, BF16),
            pltpu.VMEM((HEADS, CH, CH), BF16),
            pltpu.VMEM((GROUPS, KW), BF16),
            pltpu.VMEM((CH // TOK, TOK), jnp.int32),
            pltpu.SMEM((4,), jnp.int32),
            pltpu.VMEM(rows, F32),
            pltpu.VMEM((SPANS, PER, TOK), BF16),
            pltpu.VMEM(blocks, BF16),
            pltpu.VMEM(blocks, BF16),
            pltpu.VMEM(blocks, BF16),
            pltpu.VMEM((OWN, SPANS + LAGS - 1, PER, TOK), BF16),
            pltpu.VMEM(blocks, BF16),
            pltpu.VMEM((OWN, TOK, KW), BF16),
            pltpu.VMEM((OWN, 2, ROWS // 2, KW), BF16),
            pltpu.VMEM((OWN, 2, TOK, ROWS // 2), BF16),
            pltpu.VMEM((TOK, KW + TOK), F32),
            pltpu.VMEM((LAGS, OWN, TOK), F32),
            pltpu.VMEM((OWN, PER, TOK), F32),
            dma((12,)),
            dma((18,)),
            dma((18,)),
            dma((4,)),
            dma((4,)),
        ],
        compiler_params=pltpu.CompilerParams(
            collective_id=0, has_side_effects=True, vmem_limit_bytes=40 << 20
        ),
    )(*(pltpu.with_memory_space_constraint(arg, pltpu.HBM) for arg in args))
    return pl.pallas_call(
        finish,
        out_shape=(
            jax.ShapeDtypeStruct(rows, BF16),
            jax.ShapeDtypeStruct(rows, BF16),
            jax.ShapeDtypeStruct((GROUPS, TOK), F32),
        ),
        in_specs=[vmem] * 3,
        out_specs=(hbm,) * 3,
        scratch_shapes=[pltpu.VMEM((GROUPS, TOK), F32), dma((3,))],
        compiler_params=pltpu.CompilerParams(vmem_limit_bytes=16 << 20),
    )(*held)


def solution(mesh):
    in_specs = (
        P("ctx", "head"),
        P("ctx", "head"),
        P("ctx", "head"),
        P("ctx", "head"),
        P("head", None),
        P("head", None),
        P("head"),
        P(),
        P("head"),
    )
    out_specs = (P("ctx", "head"), P("ctx", "head"), P("head", "ctx"))
    return jax.shard_map(
        per_device, mesh=mesh, in_specs=in_specs, out_specs=out_specs, check_vma=False
    )
```

```python
import jax
import jax.numpy as jnp
from jax import lax
from jax.experimental import pallas as pl
from jax.experimental.pallas import tpu as pltpu
from jax.sharding import PartitionSpec as P

TOK = 128
SPANS = 32
HEADS = 4
CH = 1024
GROUPS = 64
PER = 16
OWN = GROUPS // SPANS
LAGS = 17
KW = LAGS * TOK
HALF = SPANS // 2
PIECE = CH // 8
ROWS = SPANS * PER
MESH = pl.DeviceIdType.MESH
F32 = jnp.float32
BF16 = jnp.bfloat16


def dot(a, b, ca, cb):
    return lax.dot_general(a, b, (((ca,), (cb,)), ((), ())), preferred_element_type=F32)


def iota(shape, dim):
    return lax.broadcasted_iota(jnp.int32, shape, dim)


def kernel(
    doc_in, go, q, k, v, w, filt, grp_in, skip_in,
    out_q, out_k, fr,
    yr, perm, conv, qv, kv, skip, own, gov, vv, wv, fv, grp, doc, fg, rem, gs, gr, xs, xr, ys, toep, amat, gt, corr, fs, gain,
    loc, ag_send, ag_recv, ex_send, ex_recv,
):
    i = lax.axis_index("ctx")
    h = lax.axis_index("head")
    up = lax.rem(h + 1, HEADS)
    down = lax.rem(h + HEADS - 1, HEADS)
    across = lax.rem(h + 2, HEADS)
    x, z, core = i // 8, lax.rem(i // 2, 4), lax.rem(i, 2)

    barrier = pltpu.get_barrier_semaphore()
    pl.semaphore_signal(barrier, inc=1, device_id={"head": up}, device_id_type=MESH)
    pl.semaphore_signal(barrier, inc=1, device_id={"head": down}, device_id_type=MESH)

    def greet(n, carry):
        pl.semaphore_signal(barrier, inc=1, device_id={"ctx": lax.rem(i + n, SPANS)}, device_id_type=MESH)
        return carry

    lax.fori_loop(1, SPANS, greet, 0)

    pairs = [(grp_in, grp), (go, own), (q, qv), (k, kv), (doc_in, doc), (filt.at[:, pl.ds(0, KW)], fv), (v, vv), (skip_in, skip)]
    for slot, block in enumerate((h, down, up, across)):
        pairs.append((w.at[:, pl.ds(pl.multiple_of(block * CH, CH), CH)], wv.at[slot]))
    loads = [pltpu.make_async_copy(src, dst, loc.at[n]) for n, (src, dst) in enumerate(pairs)]
    for load in loads:
        load.start()
    l_grp, l_own, l_q, l_k, l_doc, l_filt, l_v, l_skip = loads[:8]
    l_w = loads[8:]
    pl.semaphore_wait(barrier, SPANS + 1)

    def over_head(n, src, dst, to, first, count):
        at = pl.ds(first * PIECE, count * PIECE)
        return pltpu.make_async_remote_copy(
            src.at[:, at], dst.at[:, at], ag_send.at[n], ag_recv.at[n], device_id={"head": to}, device_id_type=MESH
        )

    first, second = range(4), range(4, 8)
    to_up = [over_head(n, own, gov.at[0], up, n, 1) for n in first]
    to_down = [over_head(n, own, gov.at[1], down, n, 1) for n in second]
    rest_up = over_head(8, own, gov.at[0], up, 4, 4)
    rest_down = over_head(9, own, gov.at[1], down, 0, 4)
    on_up = [over_head(10 + n, gov.at[0], gov.at[2], up, n, 1) for n in first]
    on_down = [over_head(10 + n, gov.at[1], gov.at[2], down, n, 1) for n in second]
    l_own.wait()
    for n in first:
        to_up[n].start()
        to_down[n].start()
    rest_up.start()
    rest_down.start()

    flips = {0: x, 1: x + 1 - 2 * lax.rem(x, 2), 2: lax.rem(x + 2, 4), 3: 3 - x}
    turns = {0: z, 1: z + 1 - 2 * lax.rem(z, 2), 2: lax.rem(z + 2, 4), 3: 3 - z}
    hops = {0: 0, 1: 1, 2: 2, 3: 1}

    def by_distance(steps):
        steps = sorted(steps, key=lambda e: -hops[e[0]] - hops[e[1]])
        return [flips[a] * 8 + turns[b] * 2 + (core if c == 0 else 1 - core) for a, b, c in steps]

    halves = (1 - x // 2, x // 2)
    steps = [(a, b, c) for a in range(4) for b in range(4) for c in range(2) if a or b or c]
    partners = by_distance(steps)
    sides = [by_distance([e for e in steps if (e[0] > 1) == far]) for far in (True, False)]

    def exchange(n, src, dst, to):
        return pltpu.make_async_remote_copy(
            src, dst, ex_send.at[n], ex_recv.at[n], device_id={"ctx": to}, device_id_type=MESH
        )

    def both(n, src, dst):
        return exchange(n, src.at[:, pl.ds(0, SPANS - 1)], dst.at[:, pl.ds(0, SPANS - 1)], i)

    l_grp.wait()
    local = grp[...] - h * GROUPS
    before = jnp.where(iota((TOK, TOK), 0) < iota((TOK, TOK), 1), 1.0, 0.0).astype(BF16)
    names = iota((GROUPS, TOK), 0)
    total = jnp.zeros((GROUPS, 1), F32)
    for b in range(CH // TOK):
        row = local[b : b + 1, :]
        hot = jnp.where(names == row, 1.0, 0.0)
        count = jnp.sum(hot * (dot(hot.astype(BF16), before, 1, 0) + total), axis=0, keepdims=True)
        total = total + jnp.sum(hot, axis=1, keepdims=True)
        rank = (row & (OWN - 1)) * ROWS + lax.shift_right_logical(row, 1) * PER + count.astype(jnp.int32)
        for r in range(CH // TOK):
            perm[r * TOK : (r + 1) * TOK, b * TOK : (b + 1) * TOK] = jnp.where(
                iota((TOK, TOK), 0) + r * TOK == rank, 1.0, 0.0
            ).astype(BF16)

    l_q.wait()
    l_k.wait()
    gated = (qv[...].astype(F32) * kv[...].astype(F32)).astype(BF16)
    for u in range(OWN):
        gs[u] = dot(perm[u * ROWS : (u + 1) * ROWS, :], gated, 1, 1).astype(BF16).reshape(SPANS, PER, TOK)
    for to in partners:
        exchange(0, gs.at[:, to], gr.at[:, i], to).start()
    gr[:, i] = gs[:, i]


    def features(block, slot, first=False):
        def tile(n, carry):
            at = pl.ds(pl.multiple_of(n * 256, 256), 256)
            part = dot(block[...], wv[slot, at, :], 1, 1)
            fg[:, at] = part if first else fg[:, at] + part
            return carry

        lax.fori_loop(0, CH // 256, tile, 0)

    l_w[0].wait()
    features(own, 0, True)

    for n in first:
        to_up[n].wait_recv()
        on_up[n].start()
        to_down[n].wait_recv()
        on_down[n].start()

    l_doc.wait()
    block = lax.shift_right_logical(iota((ROWS, TOK), 0), 4)
    ends = [doc[0]]
    for n in range(1, 4):
        ends.append(ends[-1] + doc[n])
    end = jnp.where(block < ends[0], ends[0], jnp.where(block < ends[1], ends[1], jnp.where(block < ends[2], ends[2], ends[3])))
    rem[...] = (end - block).astype(F32).astype(BF16).reshape(SPANS, PER, TOK)
    xr[:, SPANS:] = jnp.zeros((OWN, LAGS - 1, PER, TOK), BF16)
    corr[:, KW:] = jnp.zeros((TOK, TOK), F32)

    l_skip.wait()
    for u in range(OWN):
        hot = perm[pl.ds(pl.multiple_of(u * ROWS + i * PER, PER), PER), :].astype(F32)
        gain[u] = jnp.broadcast_to(jnp.sum(hot * skip[...], axis=1, keepdims=True), (PER, TOK))

    l_filt.wait()
    for u in range(OWN):
        pick = jnp.where(iota((PER, GROUPS), 1) == i * OWN + u, 1.0, 0.0).astype(BF16)
        line = dot(pick, fv[...], 1, 0)
        line = jnp.concatenate([line, jnp.zeros((PER, TOK), F32)], axis=1)
        for c in range(TOK // PER):
            turned = pltpu.roll(line, c * PER, 1, stride=1, stride_axis=0)
            toep[u, c * PER : (c + 1) * PER, :] = turned[:, :KW].astype(BF16)

    rest_up.wait_recv()
    l_w[1].wait()
    features(gov.at[0], 1)
    rest_down.wait_recv()
    l_w[2].wait()
    features(gov.at[1], 2)

    both(0, gs, gr).wait_recv()
    flip = jnp.where(iota((TOK, TOK), 0) + iota((TOK, TOK), 1) == TOK - 1, 1.0, 0.0).astype(BF16)
    for u in range(OWN):
        for p, half in enumerate(halves):
            rows = gr[u, pl.ds(half * HALF, HALF)].reshape(ROWS // 2, TOK)
            gt[u, p] = dot(flip, rows, 1, 1).astype(BF16)

    l_w[3].wait()
    l_v.wait()
    far = gov.at[2]
    for n in first:
        on_up[n].wait_recv()
        on_down[n].wait_recv()
        one, two = pl.ds(n * PIECE, PIECE), pl.ds((4 + n) * PIECE, PIECE)
        rows = jnp.concatenate([far[:, one], far[:, two]], axis=1)
        for m in range(CH // 256):
            at = slice(m * 256, (m + 1) * 256)
            part = fg[:, at] + dot(rows, jnp.concatenate([wv[3, at, one], wv[3, at, two]], axis=1), 1, 1)
            if n < 3:
                fg[:, at] = part
            else:
                conv[:, at] = (part * vv[:, at].astype(F32)).astype(BF16)

    for u in range(OWN):
        part = dot(perm[u * ROWS : (u + 1) * ROWS, :], conv[...], 1, 1)
        xs[u] = part.astype(BF16).reshape(SPANS, PER, TOK)
    for to in partners:
        exchange(1, xs.at[:, to], xr.at[:, i], to).start()
    xr[:, i] = xs[:, i]

    both(1, xs, xr).wait_recv()
    for p, (side, half) in enumerate(zip(sides, halves)):
        left = []
        for m in range(HALF):
            j = half * HALF + m
            e0 = jnp.where(j < ends[0], ends[0], jnp.where(j < ends[1], ends[1], jnp.where(j < ends[2], ends[2], ends[3])))
            left.append(e0 - j)
        for u in range(OWN):
            acc = (xr[u, pl.ds(half * HALF, HALF)].astype(F32) * gain[u][None]).reshape(ROWS // 2, TOK)
            for d in range(0, LAGS, 2):
                parts = [
                    jnp.concatenate([jnp.where(left[m] > e, xr[u, half * HALF + (e + m)], jnp.zeros((PER, TOK), BF16)) for m in range(HALF)], axis=0)
                    for e in range(d, min(d + 2, LAGS))
                ]
                at = slice(d * TOK, (d + len(parts)) * TOK)
                part = jnp.concatenate(parts, axis=1)
                amat[u, p, :, at] = part
                acc = acc + dot(part, toep[u, :, at], 1, 1)
            ys[u, pl.ds(half * HALF, HALF)] = acc.astype(BF16).reshape(HALF, PER, TOK)
        for to in side:
            exchange(2, ys.at[:, to], yr.at[:, i], to).start()
    yr[:, i] = ys[:, i]

    for u in range(OWN):
        corr[:, :KW] = dot(gt[u, 0], amat[u, 0], 1, 0) + dot(gt[u, 1], amat[u, 1], 1, 0)
        acc = jnp.zeros((PER, KW + TOK), F32)
        for c in range(TOK // PER):
            acc = acc + pltpu.roll(corr[c * PER : (c + 1) * PER, :], 1 + c * PER, 1, stride=1, stride_axis=0)
        line = jnp.sum(acc, axis=0, keepdims=True)
        for d in range(LAGS):
            fs[d, u : u + 1, :] = line[:, (d + 1) * TOK : (d + 2) * TOK]
    for side in sides:
        for to in side:

            @pl.when(to < LAGS)
            def _(to=to):
                exchange(3, fs.at[to], fr.at[i], to).start()

    both(2, ys, yr).wait_recv()
    for u in range(OWN):
        for n in range(CH // 256):
            at = slice(n * 256, (n + 1) * 256)
            part = dot(yr[u].reshape(ROWS, TOK), perm[u * ROWS : (u + 1) * ROWS, at], 0, 0)
            if u == 0:
                fg[:, at] = part
            else:
                grad = fg[:, at] + part
                out_q[:, at] = (grad * kv[:, at].astype(F32)).astype(BF16)
                out_k[:, at] = (grad * qv[:, at].astype(F32)).astype(BF16)

    @pl.when(i < LAGS)
    def _():
        fr[i] = fs[i]
        exchange(3, fr.at[pl.ds(0, SPANS - 1)], fr.at[pl.ds(0, SPANS - 1)], i).wait_recv()
        exchange(3, fs.at[pl.ds(0, LAGS - 1)], fr.at[pl.ds(0, LAGS - 1)], i).wait_send()

    @pl.when(i >= LAGS)
    def _():
        fr[...] = jnp.zeros(fr.shape, F32)
        exchange(3, fs, fr.at[pl.ds(0, LAGS)], i).wait_send()

    for copy in (*to_up, *to_down, rest_up, rest_down, *on_up, *on_down):
        copy.wait_send()
    both(0, gs, gr).wait_send()
    both(1, xs, xr).wait_send()
    both(2, ys, yr).wait_send()


def finish(out_q, out_k, fr, gq, gk, gf, out_f, sem):
    copies = [pltpu.make_async_copy(src, dst, sem.at[n]) for n, (src, dst) in enumerate(((out_q, gq), (out_k, gk), (out_f, gf)))]
    copies[0].start()
    copies[1].start()
    for t in range(SPANS):
        out_f[t * OWN : (t + 1) * OWN, :] = fr[t]
    copies[2].start()
    for copy in copies:
        copy.wait()


def per_device(
    query_proj, key_proj, value_proj, grad_out, out_proj, filters, skip_gain, doc_lengths, group_of
):
    hbm = pl.BlockSpec(memory_space=pltpu.HBM)
    vmem = pl.BlockSpec(memory_space=pltpu.VMEM)
    dma = pltpu.SemaphoreType.DMA
    blocks = (OWN, SPANS, PER, TOK)
    rows = (TOK, CH)
    args = (
        doc_lengths, grad_out, query_proj, key_proj, value_proj, out_proj, filters,
        group_of.reshape(CH // TOK, TOK), skip_gain.reshape(1, CH),
    )
    held = pl.pallas_call(
        kernel,
        out_shape=(
            jax.ShapeDtypeStruct(rows, BF16),
            jax.ShapeDtypeStruct(rows, BF16),
            jax.ShapeDtypeStruct((SPANS, OWN, TOK), F32),
        ),
        in_specs=[hbm] * 9,
        out_specs=(vmem,) * 3,
        scratch_shapes=[
            pltpu.VMEM(blocks, BF16),
            pltpu.VMEM((CH, CH), BF16),
            pltpu.VMEM(rows, BF16),
            pltpu.VMEM(rows, BF16),
            pltpu.VMEM(rows, BF16),
            pltpu.VMEM((1, CH), F32),
            pltpu.VMEM(rows, BF16),
            pltpu.VMEM((HEADS - 1, *rows), BF16),
            pltpu.VMEM(rows, BF16),
            pltpu.VMEM((HEADS, CH, CH), BF16),
            pltpu.VMEM((GROUPS, KW), BF16),
            pltpu.VMEM((CH // TOK, TOK), jnp.int32),
            pltpu.SMEM((4,), jnp.int32),
            pltpu.VMEM(rows, F32),
            pltpu.VMEM((SPANS, PER, TOK), BF16),
            pltpu.VMEM(blocks, BF16),
            pltpu.VMEM(blocks, BF16),
            pltpu.VMEM(blocks, BF16),
            pltpu.VMEM((OWN, SPANS + LAGS - 1, PER, TOK), BF16),
            pltpu.VMEM(blocks, BF16),
            pltpu.VMEM((OWN, TOK, KW), BF16),
            pltpu.VMEM((OWN, 2, ROWS // 2, KW), BF16),
            pltpu.VMEM((OWN, 2, TOK, ROWS // 2), BF16),
            pltpu.VMEM((TOK, KW + TOK), F32),
            pltpu.VMEM((LAGS, OWN, TOK), F32),
            pltpu.VMEM((OWN, PER, TOK), F32),
            dma((12,)),
            dma((18,)),
            dma((18,)),
            dma((4,)),
            dma((4,)),
        ],
        compiler_params=pltpu.CompilerParams(
            collective_id=0, has_side_effects=True, vmem_limit_bytes=40 << 20
        ),
    )(*(pltpu.with_memory_space_constraint(arg, pltpu.HBM) for arg in args))
    return pl.pallas_call(
        finish,
        out_shape=(
            jax.ShapeDtypeStruct(rows, BF16),
            jax.ShapeDtypeStruct(rows, BF16),
            jax.ShapeDtypeStruct((GROUPS, TOK), F32),
        ),
        in_specs=[vmem] * 3,
        out_specs=(hbm,) * 3,
        scratch_shapes=[pltpu.VMEM((GROUPS, TOK), F32), dma((3,))],
        compiler_params=pltpu.CompilerParams(vmem_limit_bytes=16 << 20),
    )(*held)


def solution(mesh):
    in_specs = (
        P("ctx", "head"),
        P("ctx", "head"),
        P("ctx", "head"),
        P("ctx", "head"),
        P("head", None),
        P("head", None),
        P("head"),
        P(),
        P("head"),
    )
    out_specs = (P("ctx", "head"), P("ctx", "head"), P("head", "ctx"))
    return jax.shard_map(
        per_device, mesh=mesh, in_specs=in_specs, out_specs=out_specs, check_vma=False
    )
```

```python
import jax
import jax.numpy as jnp
from jax import lax
from jax.experimental import pallas as pl
from jax.experimental.pallas import tpu as pltpu
from jax.sharding import PartitionSpec as P

TOK = 128
SPANS = 32
HEADS = 4
CH = 1024
GROUPS = 64
PER = 16
OWN = GROUPS // SPANS
LAGS = 17
KW = LAGS * TOK
HALF = SPANS // 2
PIECE = CH // 8
ROWS = SPANS * PER
MESH = pl.DeviceIdType.MESH
F32 = jnp.float32
BF16 = jnp.bfloat16


def dot(a, b, ca, cb):
    return lax.dot_general(a, b, (((ca,), (cb,)), ((), ())), preferred_element_type=F32)


def iota(shape, dim):
    return lax.broadcasted_iota(jnp.int32, shape, dim)


def kernel(
    doc_in, go, q, k, v, w, filt, grp_in, skip_in,
    out_q, out_k, fr,
    yr, perm, conv, qv, kv, skip, own, gov, vv, wv, fv, grp, doc, fg, gs, gr, xs, xr, ys, toep, amat, gt, corr, fs, gain,
    loc, ag_send, ag_recv, ex_send, ex_recv,
):
    i = lax.axis_index("ctx")
    h = lax.axis_index("head")
    up = lax.rem(h + 1, HEADS)
    down = lax.rem(h + HEADS - 1, HEADS)
    across = lax.rem(h + 2, HEADS)
    x, z, core = i // 8, lax.rem(i // 2, 4), lax.rem(i, 2)

    barrier = pltpu.get_barrier_semaphore()
    pl.semaphore_signal(barrier, inc=1, device_id={"head": up}, device_id_type=MESH)
    pl.semaphore_signal(barrier, inc=1, device_id={"head": down}, device_id_type=MESH)

    def greet(n, carry):
        pl.semaphore_signal(barrier, inc=1, device_id={"ctx": lax.rem(i + n, SPANS)}, device_id_type=MESH)
        return carry

    lax.fori_loop(1, SPANS, greet, 0)

    pairs = [(grp_in, grp), (go, own), (q, qv), (k, kv), (doc_in, doc), (filt.at[:, pl.ds(0, KW)], fv), (v, vv), (skip_in, skip)]
    for slot, block in enumerate((h, down, up, across)):
        pairs.append((w.at[:, pl.ds(pl.multiple_of(block * CH, CH), CH)], wv.at[slot]))
    loads = [pltpu.make_async_copy(src, dst, loc.at[n]) for n, (src, dst) in enumerate(pairs)]
    for load in loads:
        load.start()
    l_grp, l_own, l_q, l_k, l_doc, l_filt, l_v, l_skip = loads[:8]
    l_w = loads[8:]
    pl.semaphore_wait(barrier, SPANS + 1)

    def over_head(n, src, dst, to, first, count):
        at = pl.ds(first * PIECE, count * PIECE)
        return pltpu.make_async_remote_copy(
            src.at[:, at], dst.at[:, at], ag_send.at[n], ag_recv.at[n], device_id={"head": to}, device_id_type=MESH
        )

    first, second = range(4), range(4, 8)
    to_up = [over_head(n, own, gov.at[0], up, n, 1) for n in first]
    to_down = [over_head(n, own, gov.at[1], down, n, 1) for n in second]
    rest_up = over_head(8, own, gov.at[0], up, 4, 4)
    rest_down = over_head(9, own, gov.at[1], down, 0, 4)
    on_up = [over_head(10 + n, gov.at[0], gov.at[2], up, n, 1) for n in first]
    on_down = [over_head(10 + n, gov.at[1], gov.at[2], down, n, 1) for n in second]
    l_own.wait()
    for n in first:
        to_up[n].start()
        to_down[n].start()
    rest_up.start()
    rest_down.start()

    flips = {0: x, 1: x + 1 - 2 * lax.rem(x, 2), 2: lax.rem(x + 2, 4), 3: 3 - x}
    turns = {0: z, 1: z + 1 - 2 * lax.rem(z, 2), 2: lax.rem(z + 2, 4), 3: 3 - z}
    hops = {0: 0, 1: 1, 2: 2, 3: 1}

    def by_distance(steps):
        steps = sorted(steps, key=lambda e: -hops[e[0]] - hops[e[1]])
        return [flips[a] * 8 + turns[b] * 2 + (core if c == 0 else 1 - core) for a, b, c in steps]

    halves = (1 - x // 2, x // 2)
    steps = [(a, b, c) for a in range(4) for b in range(4) for c in range(2) if a or b or c]
    partners = by_distance(steps)
    sides = [by_distance([e for e in steps if (e[0] > 1) == far]) for far in (True, False)]

    def exchange(n, src, dst, to):
        return pltpu.make_async_remote_copy(
            src, dst, ex_send.at[n], ex_recv.at[n], device_id={"ctx": to}, device_id_type=MESH
        )

    def both(n, src, dst):
        return exchange(n, src.at[:, pl.ds(0, SPANS - 1)], dst.at[:, pl.ds(0, SPANS - 1)], i)

    l_grp.wait()
    local = grp[...] - h * GROUPS
    before = jnp.where(iota((TOK, TOK), 0) < iota((TOK, TOK), 1), 1.0, 0.0).astype(BF16)
    names = iota((GROUPS, TOK), 0)
    total = jnp.zeros((GROUPS, 1), F32)
    for b in range(CH // TOK):
        row = local[b : b + 1, :]
        hot = jnp.where(names == row, 1.0, 0.0)
        count = jnp.sum(hot * (dot(hot.astype(BF16), before, 1, 0) + total), axis=0, keepdims=True)
        total = total + jnp.sum(hot, axis=1, keepdims=True)
        rank = (row & (OWN - 1)) * ROWS + lax.shift_right_logical(row, 1) * PER + count.astype(jnp.int32)
        for r in range(CH // TOK):
            perm[r * TOK : (r + 1) * TOK, b * TOK : (b + 1) * TOK] = jnp.where(
                iota((TOK, TOK), 0) + r * TOK == rank, 1.0, 0.0
            ).astype(BF16)

    l_q.wait()
    l_k.wait()
    gated = (qv[...].astype(F32) * kv[...].astype(F32)).astype(BF16)
    for u in range(OWN):
        gs[u] = dot(perm[u * ROWS : (u + 1) * ROWS, :], gated, 1, 1).astype(BF16).reshape(SPANS, PER, TOK)
    for to in partners:
        exchange(0, gs.at[:, to], gr.at[:, i], to).start()
    gr[:, i] = gs[:, i]


    def features(block, slot, first=False):
        def tile(n, carry):
            at = pl.ds(pl.multiple_of(n * 256, 256), 256)
            part = dot(block[...], wv[slot, at, :], 1, 1)
            fg[:, at] = part if first else fg[:, at] + part
            return carry

        lax.fori_loop(0, CH // 256, tile, 0)

    l_w[0].wait()
    features(own, 0, True)

    for n in first:
        to_up[n].wait_recv()
        on_up[n].start()
        to_down[n].wait_recv()
        on_down[n].start()

    l_doc.wait()
    ends = [doc[0]]
    for n in range(1, 4):
        ends.append(ends[-1] + doc[n])
    xr[:, SPANS:] = jnp.zeros((OWN, LAGS - 1, PER, TOK), BF16)
    corr[:, KW:] = jnp.zeros((TOK, TOK), F32)

    l_skip.wait()
    for u in range(OWN):
        hot = perm[pl.ds(pl.multiple_of(u * ROWS + i * PER, PER), PER), :].astype(F32)
        gain[u] = jnp.broadcast_to(jnp.sum(hot * skip[...], axis=1, keepdims=True), (PER, TOK))

    l_filt.wait()
    for u in range(OWN):
        pick = jnp.where(iota((PER, GROUPS), 1) == i * OWN + u, 1.0, 0.0).astype(BF16)
        line = dot(pick, fv[...], 1, 0)
        line = jnp.concatenate([line, jnp.zeros((PER, TOK), F32)], axis=1)
        for c in range(TOK // PER):
            turned = pltpu.roll(line, c * PER, 1, stride=1, stride_axis=0)
            toep[u, c * PER : (c + 1) * PER, :] = turned[:, :KW].astype(BF16)

    rest_up.wait_recv()
    l_w[1].wait()
    features(gov.at[0], 1)
    rest_down.wait_recv()
    l_w[2].wait()
    features(gov.at[1], 2)

    both(0, gs, gr).wait_recv()
    flip = jnp.where(iota((TOK, TOK), 0) + iota((TOK, TOK), 1) == TOK - 1, 1.0, 0.0).astype(BF16)
    for u in range(OWN):
        for p, half in enumerate(halves):
            rows = gr[u, pl.ds(half * HALF, HALF)].reshape(ROWS // 2, TOK)
            gt[u, p] = dot(flip, rows, 1, 1).astype(BF16)

    l_w[3].wait()
    l_v.wait()
    far = gov.at[2]
    for n in first:
        on_up[n].wait_recv()
        on_down[n].wait_recv()
        one, two = pl.ds(n * PIECE, PIECE), pl.ds((4 + n) * PIECE, PIECE)
        rows = jnp.concatenate([far[:, one], far[:, two]], axis=1)
        for m in range(CH // 256):
            at = slice(m * 256, (m + 1) * 256)
            part = fg[:, at] + dot(rows, jnp.concatenate([wv[3, at, one], wv[3, at, two]], axis=1), 1, 1)
            if n < 3:
                fg[:, at] = part
            else:
                conv[:, at] = (part * vv[:, at].astype(F32)).astype(BF16)

    for u in range(OWN):
        part = dot(perm[u * ROWS : (u + 1) * ROWS, :], conv[...], 1, 1)
        xs[u] = part.astype(BF16).reshape(SPANS, PER, TOK)
    for to in partners:
        exchange(1, xs.at[:, to], xr.at[:, i], to).start()
    xr[:, i] = xs[:, i]

    both(1, xs, xr).wait_recv()
    for p, (side, half) in enumerate(zip(sides, halves)):
        left = []
        for m in range(HALF):
            j = half * HALF + m
            e0 = jnp.where(j < ends[0], ends[0], jnp.where(j < ends[1], ends[1], jnp.where(j < ends[2], ends[2], ends[3])))
            left.append(e0 - j)
        for u in range(OWN):
            acc = (xr[u, pl.ds(half * HALF, HALF)].astype(F32) * gain[u][None]).reshape(ROWS // 2, TOK)
            for d in range(0, LAGS, 2):
                parts = [
                    jnp.concatenate([jnp.where(left[m] > e, xr[u, half * HALF + (e + m)], jnp.zeros((PER, TOK), BF16)) for m in range(HALF)], axis=0)
                    for e in range(d, min(d + 2, LAGS))
                ]
                at = slice(d * TOK, (d + len(parts)) * TOK)
                part = jnp.concatenate(parts, axis=1)
                amat[u, p, :, at] = part
                acc = acc + dot(part, toep[u, :, at], 1, 1)
            ys[u, pl.ds(half * HALF, HALF)] = acc.astype(BF16).reshape(HALF, PER, TOK)
        for to in side:
            exchange(2, ys.at[:, to], yr.at[:, i], to).start()
    yr[:, i] = ys[:, i]

    for u in range(OWN):
        corr[:, :KW] = dot(gt[u, 0], amat[u, 0], 1, 0) + dot(gt[u, 1], amat[u, 1], 1, 0)
        acc = jnp.zeros((PER, KW + TOK), F32)
        for c in range(TOK // PER):
            acc = acc + pltpu.roll(corr[c * PER : (c + 1) * PER, :], 1 + c * PER, 1, stride=1, stride_axis=0)
        line = jnp.sum(acc, axis=0, keepdims=True)
        for d in range(LAGS):
            fs[d, u : u + 1, :] = line[:, (d + 1) * TOK : (d + 2) * TOK]
    for side in sides:
        for to in side:

            @pl.when(to < LAGS)
            def _(to=to):
                exchange(3, fs.at[to], fr.at[i], to).start()

    both(2, ys, yr).wait_recv()
    for u in range(OWN):
        for n in range(CH // 256):
            at = slice(n * 256, (n + 1) * 256)
            part = dot(yr[u].reshape(ROWS, TOK), perm[u * ROWS : (u + 1) * ROWS, at], 0, 0)
            if u == 0:
                fg[:, at] = part
            else:
                grad = fg[:, at] + part
                out_q[:, at] = (grad * kv[:, at].astype(F32)).astype(BF16)
                out_k[:, at] = (grad * qv[:, at].astype(F32)).astype(BF16)

    @pl.when(i < LAGS)
    def _():
        fr[i] = fs[i]
        exchange(3, fr.at[pl.ds(0, SPANS - 1)], fr.at[pl.ds(0, SPANS - 1)], i).wait_recv()
        exchange(3, fs.at[pl.ds(0, LAGS - 1)], fr.at[pl.ds(0, LAGS - 1)], i).wait_send()

    @pl.when(i >= LAGS)
    def _():
        fr[...] = jnp.zeros(fr.shape, F32)
        exchange(3, fs, fr.at[pl.ds(0, LAGS)], i).wait_send()

    for copy in (*to_up, *to_down, rest_up, rest_down, *on_up, *on_down):
        copy.wait_send()
    both(0, gs, gr).wait_send()
    both(1, xs, xr).wait_send()
    both(2, ys, yr).wait_send()


def finish(out_q, out_k, fr, gq, gk, gf, out_f, sem):
    copies = [pltpu.make_async_copy(src, dst, sem.at[n]) for n, (src, dst) in enumerate(((out_q, gq), (out_k, gk), (out_f, gf)))]
    copies[0].start()
    copies[1].start()
    for t in range(SPANS):
        out_f[t * OWN : (t + 1) * OWN, :] = fr[t]
    copies[2].start()
    for copy in copies:
        copy.wait()


def per_device(
    query_proj, key_proj, value_proj, grad_out, out_proj, filters, skip_gain, doc_lengths, group_of
):
    hbm = pl.BlockSpec(memory_space=pltpu.HBM)
    vmem = pl.BlockSpec(memory_space=pltpu.VMEM)
    dma = pltpu.SemaphoreType.DMA
    blocks = (OWN, SPANS, PER, TOK)
    rows = (TOK, CH)
    args = (
        doc_lengths, grad_out, query_proj, key_proj, value_proj, out_proj, filters,
        group_of.reshape(CH // TOK, TOK), skip_gain.reshape(1, CH),
    )
    held = pl.pallas_call(
        kernel,
        out_shape=(
            jax.ShapeDtypeStruct(rows, BF16),
            jax.ShapeDtypeStruct(rows, BF16),
            jax.ShapeDtypeStruct((SPANS, OWN, TOK), F32),
        ),
        in_specs=[hbm] * 9,
        out_specs=(vmem,) * 3,
        scratch_shapes=[
            pltpu.VMEM(blocks, BF16),
            pltpu.VMEM((CH, CH), BF16),
            pltpu.VMEM(rows, BF16),
            pltpu.VMEM(rows, BF16),
            pltpu.VMEM(rows, BF16),
            pltpu.VMEM((1, CH), F32),
            pltpu.VMEM(rows, BF16),
            pltpu.VMEM((HEADS - 1, *rows), BF16),
            pltpu.VMEM(rows, BF16),
            pltpu.VMEM((HEADS, CH, CH), BF16),
            pltpu.VMEM((GROUPS, KW), BF16),
            pltpu.VMEM((CH // TOK, TOK), jnp.int32),
            pltpu.SMEM((4,), jnp.int32),
            pltpu.VMEM(rows, F32),
            pltpu.VMEM(blocks, BF16),
            pltpu.VMEM(blocks, BF16),
            pltpu.VMEM(blocks, BF16),
            pltpu.VMEM((OWN, SPANS + LAGS - 1, PER, TOK), BF16),
            pltpu.VMEM(blocks, BF16),
            pltpu.VMEM((OWN, TOK, KW), BF16),
            pltpu.VMEM((OWN, 2, ROWS // 2, KW), BF16),
            pltpu.VMEM((OWN, 2, TOK, ROWS // 2), BF16),
            pltpu.VMEM((TOK, KW + TOK), F32),
            pltpu.VMEM((LAGS, OWN, TOK), F32),
            pltpu.VMEM((OWN, PER, TOK), F32),
            dma((12,)),
            dma((18,)),
            dma((18,)),
            dma((4,)),
            dma((4,)),
        ],
        compiler_params=pltpu.CompilerParams(
            collective_id=0, has_side_effects=True, vmem_limit_bytes=40 << 20
        ),
    )(*(pltpu.with_memory_space_constraint(arg, pltpu.HBM) for arg in args))
    return pl.pallas_call(
        finish,
        out_shape=(
            jax.ShapeDtypeStruct(rows, BF16),
            jax.ShapeDtypeStruct(rows, BF16),
            jax.ShapeDtypeStruct((GROUPS, TOK), F32),
        ),
        in_specs=[vmem] * 3,
        out_specs=(hbm,) * 3,
        scratch_shapes=[pltpu.VMEM((GROUPS, TOK), F32), dma((3,))],
        compiler_params=pltpu.CompilerParams(vmem_limit_bytes=16 << 20),
    )(*held)


def solution(mesh):
    in_specs = (
        P("ctx", "head"),
        P("ctx", "head"),
        P("ctx", "head"),
        P("ctx", "head"),
        P("head", None),
        P("head", None),
        P("head"),
        P(),
        P("head"),
    )
    out_specs = (P("ctx", "head"), P("ctx", "head"), P("head", "ctx"))
    return jax.shard_map(
        per_device, mesh=mesh, in_specs=in_specs, out_specs=out_specs, check_vma=False
    )
```
